256 devices in a mesh: blk: 8 (over x, core), seq: 32 (over y, z).
Axes of the slice: x: 4, y: 4, z: 8, core: 2. Of those that a mesh axis runs over, the one named last changes fastest.
Arguments:
- patches: bfloat16 [8, 8192, 1408], P('blk', 'seq'), may hold values from -12 to 12
- group_segments: int32 [8, 2048], P('blk', 'seq'), may hold values from 0 to 63, never falling along the last dimension, each value on 1 to 64 neighbouring positions
- cached_keyval: bfloat16 [8, 8192, 2816], P('blk', 'seq'), may hold values from -90 to 90
- recompute_rows: int32 [8, 32, 25], P('blk', 'seq'), may hold values from 0 to 255, as said below
- query_weight: bfloat16 [1408, 1408], P(None, 'seq'), may hold values from -0.15625 to 0.15625
- keyval_weight: bfloat16 [1408, 2816], P(None, 'seq'), may hold values from -0.15625 to 0.15625
- output_weight: bfloat16 [1408, 1408], P('seq'), may hold values from -0.15625 to 0.15625
- expand_weight: bfloat16 [1408, 6144], P(None, 'blk'), may hold values from -0.15625 to 0.15625
- reduce_weight: bfloat16 [6144, 1408], P('blk'), may hold values from -0.078125 to 0.078125
- merge_weight: bfloat16 [5632, 2048], P(None, 'blk'), may hold values from -0.078125 to 0.078125
- owners: int32 [32, 512], P('seq'), may hold values from 0 to 31, as said below
Outputs:
- routed: bfloat16 [32, 32, 48, 2048], P('seq', None, None, 'blk')
The draws below stay inside these ranges and needn't reach their ends.
Inputs may be any that keep to these rules, and one draw needn't show every extreme that they name: `group_segments`: segment numbers never fall along a pack; a segment covers 1 to 64 groups, one segment exactly 64. recompute_rows[p, s, :] names 25 different patches of block s of pack p, as row numbers within that block of 256 patches. `owners`: at most 48 of the listing indices of one source share an owner, and one owner has exactly 48 of them at every source.
All inputs are finite; a program needn't handle non-finite values.
Results may differ from the reference program's by a relative error of at most 0.019.
Values may be sent and summed in bfloat16 or wider, within the bound.
No kernel may reach another device: no remote copies, remote signals or barrier semaphores. Data moves between devices by JAX's collectives and lax.ppermute only.
A program may use at most 128 MiB of HBM per device.

```python
import math
import jax
import jax.numpy as jnp
import numpy as np
from jax import lax

D = 1408
HEADS = 16
HEAD = 88
FF = 6144
OUT = 2048
ROWS = 256
NPACK = 8
PACK = 8192
MROWS = 64
RECOMP = 25
CAP = 48
N_BLK = 8
N_SEQ = 32


def draw_patches(key, part):
    key_base, key_rows, key_columns = jax.random.split(key, 3)
    full_shape = (NPACK, PACK, D)
    noise = jnp.clip(jax.random.normal(key_base, full_shape, jnp.float32), -4.0, 4.0)
    row_scale = jnp.exp(jax.random.uniform(key_rows, (NPACK, PACK, 1), jnp.float32, math.log(0.3), math.log(3.0)))
    column_scale = jnp.exp(jax.random.uniform(key_columns, (D,), jnp.float32, math.log(0.3), math.log(3.0)))
    return (0.15 * noise * row_scale * column_scale).astype(jnp.bfloat16)


def draw_cached_keyval(key, part):
    key_base = jax.random.fold_in(key, 0)
    full_shape = (NPACK, PACK, 2 * D)
    return jnp.clip(jax.random.normal(key_base, full_shape, jnp.float32), -4.0, 4.0).astype(jnp.bfloat16)


def draw_recompute_rows(key, part):
    block_keys = jax.random.split(key, NPACK * N_SEQ)
    chosen = jax.vmap(lambda single: jax.random.permutation(single, ROWS)[:RECOMP])(block_keys)
    return chosen.reshape(NPACK, N_SEQ, RECOMP).astype(jnp.int32)


def draw_owners(key, part):
    listing_count = NPACK * MROWS
    favorite = jax.random.randint(jax.random.fold_in(key, 7), (), 0, N_SEQ).astype(jnp.int32)

    def one_source(single):
        key_slots, key_shuffle = jax.random.split(single)
        chosen = jax.random.permutation(key_slots, (N_SEQ - 1) * CAP)[:listing_count - CAP].astype(jnp.int32)
        others = chosen // CAP
        others = others + (others >= favorite).astype(jnp.int32)
        listing = jnp.concatenate([jnp.full((CAP,), favorite, jnp.int32), others])
        shuffle = jax.random.permutation(key_shuffle, listing_count)
        return listing[shuffle]
    source_keys = jax.random.split(jax.random.fold_in(key, 11), N_SEQ)
    return jax.vmap(one_source)(source_keys).astype(jnp.int32)


def shard_levels(key, shape, shards, smallest, top_value):
    level, own = 1.0, jax.random.fold_in(key, 6)
    for dim, parts in shards:
        heights = jnp.exp(jax.random.uniform(jax.random.fold_in(own, dim), (parts,), jnp.float32, smallest / len(shards), top_value / len(shards)))
        level = level * jnp.repeat(heights, shape[dim] // parts).reshape([-1 if axis == dim else 1 for axis in range(len(shape))])
    return level


def profile(amount, total, limit, lean):
    portions = [(1 << 20) // math.isqrt(grade ** lean) + 1 for grade in range(2, amount + 1)]
    surplus, holding = total - limit - (amount - 1), [1] * (amount - 1)
    while surplus > 0:
        candidates = [i for i in range(amount - 1) if holding[i] < limit]
        pool, remaining = sum([portions[i] for i in candidates]), surplus
        for i in candidates:
            addition = min(limit - holding[i], max(1, remaining * portions[i] // pool), surplus)
            holding[i] = holding[i] + addition
            surplus = surplus - addition
    return np.array([limit] + holding)


def uneven_parts(key, amount, total, most, lean):
    if amount == 2:
        one = jax.random.randint(key, (), max(1, total - most), min(most, total - 1) + 1)
        return jnp.stack([one, total - one])
    lengths = jnp.asarray(profile(amount, total, most, lean), jnp.int32)
    couples = (amount - 1) // 2
    source_of, receiver = lengths[1:1 + 2 * couples:2], lengths[2:2 + 2 * couples:2]
    margin = jnp.minimum(source_of - 1, most - receiver)
    moved = jax.random.randint(jax.random.fold_in(key, 1), (couples,), 0, 1 << 20) % (margin + 1)
    lengths = lengths.at[1:1 + 2 * couples:2].set(source_of - moved).at[2:2 + 2 * couples:2].set(receiver + moved)
    return lengths[jax.random.permutation(jax.random.fold_in(key, 2), amount)]


def scatter_about(key, extent, spread, reach, shards=(), held_as=jnp.bfloat16):
    entries = jax.random.normal(key, extent, jnp.float32) * spread
    if len(shards) > 0:
        entries = shard_levels(key, extent, shards, -0.22, 0.18) * entries
    return jnp.clip(entries, min=-reach, max=reach).astype(held_as)


def setup_inputs(seed: int = 0) -> dict:
    splits = jax.random.split(jax.random.key(seed), 12)
    patches = draw_patches(jax.random.fold_in(splits[11], 71), 0)
    group_segments = jax.vmap(lambda own: jnp.searchsorted(jnp.cumsum(uneven_parts(own, 2 * N_SEQ, PACK // 4, MROWS, 0)), jnp.arange(PACK // 4), side="right"))(jax.random.split(splits[1], NPACK)).reshape((NPACK, PACK // 4)).astype(jnp.int32)
    cached_keyval = draw_cached_keyval(jax.random.fold_in(splits[11], 71), 0)
    recompute_rows = draw_recompute_rows(jax.random.fold_in(splits[11], 71), 0)
    query_weight = scatter_about(splits[4], (D, D), D ** -0.5, 0.15625, ((1, 32),))
    keyval_weight = scatter_about(splits[5], (D, 2 * D), D ** -0.5, 0.15625, ((1, 32),))
    output_weight = scatter_about(splits[6], (D, D), D ** -0.5, 0.15625, ((0, 32),))
    expand_weight = scatter_about(splits[7], (D, FF), D ** -0.5, 0.15625, ((1, 8),))
    reduce_weight = scatter_about(splits[8], (FF, D), FF ** -0.5, 0.078125, ((0, 8),))
    merge_weight = scatter_about(splits[9], (4 * D, OUT), (4 * D) ** -0.5, 0.078125, ((1, 8),))
    owners = draw_owners(jax.random.fold_in(splits[11], 71), 0)
    return dict(patches=patches, group_segments=group_segments, cached_keyval=cached_keyval, recompute_rows=recompute_rows, query_weight=query_weight, keyval_weight=keyval_weight, output_weight=output_weight, expand_weight=expand_weight, reduce_weight=reduce_weight, merge_weight=merge_weight, owners=owners)


def layer_norm(values):
    average = lax.optimization_barrier(jnp.mean(values, axis=-1, keepdims=True))
    centered = values - average
    variance = lax.optimization_barrier(jnp.mean(centered * centered, axis=-1, keepdims=True))
    return centered * lax.rsqrt(variance + 1e-06)

def attend(queries, keyval, query_tag, key_tag):
    feature_count = queries.shape[1]
    query_heads = queries.astype(jnp.float32).reshape(queries.shape[0], HEADS, HEAD)
    key_rows = keyval[:, :feature_count].astype(jnp.float32).reshape(keyval.shape[0], HEADS, HEAD)
    value_rows = keyval[:, feature_count:].astype(jnp.float32).reshape(keyval.shape[0], HEADS, HEAD)
    scores = jnp.einsum('qhd,khd->hqk', query_heads, key_rows) * (1.0 / math.sqrt(HEAD))
    allowed = query_tag[:, None] == key_tag[None, :]
    scores = jnp.where(allowed[None], scores, -1e+30)
    highest = lax.optimization_barrier(jnp.max(scores, axis=-1, keepdims=True))
    raised = jnp.exp(scores - highest)
    totals = lax.optimization_barrier(jnp.sum(raised, axis=-1))
    weights = raised.astype(jnp.bfloat16)
    context = jnp.einsum('hqk,khd->qhd', weights.astype(jnp.float32), value_rows)
    context = context / jnp.transpose(totals)[:, :, None]
    return context.reshape(queries.shape[0], feature_count).astype(jnp.bfloat16)

def attend_pack(operands):
    queries, padded_keyval, padded_tag, segment_tag = operands

    def attend_block(source):
        offset = source * ROWS
        block_queries = lax.dynamic_slice_in_dim(queries, offset, ROWS, 0)
        window = lax.dynamic_slice_in_dim(padded_keyval, offset, 3 * ROWS, 0)
        window_tag = lax.dynamic_slice_in_dim(padded_tag, offset, 3 * ROWS, 0)
        block_tag = lax.dynamic_slice_in_dim(segment_tag, offset, ROWS, 0)
        return attend(block_queries, window, block_tag, window_tag)
    return lax.map(attend_block, jnp.arange(N_SEQ, dtype=jnp.int32)).reshape(PACK, D)

def make_tail(expand_weight, reduce_weight, merge_weight):

    def tail_pack(stream):
        feedforward_in = layer_norm(stream.astype(jnp.float32)).astype(jnp.bfloat16)
        hidden = jax.nn.gelu(jnp.dot(feedforward_in, expand_weight, preferred_element_type=jnp.float32), approximate=False).astype(jnp.bfloat16)
        sliced = hidden.astype(jnp.float32).reshape(PACK, N_BLK, FF // N_BLK)
        reduce_parts = reduce_weight.astype(jnp.float32).reshape(N_BLK, FF // N_BLK, D)
        partial_value = jnp.einsum('rjf,jfd->rjd', sliced, reduce_parts).astype(jnp.bfloat16)
        feedforward = lax.optimization_barrier(jnp.sum(partial_value.astype(jnp.float32), axis=1))
        combined = stream.astype(jnp.float32) + feedforward
        merged = layer_norm(combined).reshape(PACK // 4, 4 * D).astype(jnp.bfloat16)
        return jnp.dot(merged, merge_weight, preferred_element_type=jnp.float32).astype(jnp.bfloat16)
    return tail_pack

def dispatch_rows(listing, destination):
    indicator = (destination[:, None] == jnp.arange(N_SEQ, dtype=jnp.int32)[None, :]).astype(jnp.int32)
    earlier = jnp.cumsum(indicator, axis=0, dtype=jnp.int32) - indicator
    position = lax.optimization_barrier(jnp.sum(earlier * indicator, axis=1)).astype(jnp.int32)
    slot_index = destination * CAP + position
    placed = jnp.zeros((N_SEQ * CAP, OUT), jnp.bfloat16).at[slot_index].set(listing)
    return placed.reshape(N_SEQ, CAP, OUT)

def reference(patches, group_segments, cached_keyval, recompute_rows, query_weight, keyval_weight, output_weight, expand_weight, reduce_weight, merge_weight, owners):
    stream_in = patches.astype(jnp.float32)
    attention_in = layer_norm(stream_in).astype(jnp.bfloat16)
    block_start = (jnp.arange(N_SEQ, dtype=jnp.int32) * ROWS)[None, :, None]
    where_rows = (recompute_rows + block_start).reshape(NPACK, N_SEQ * RECOMP).astype(jnp.int32)
    gathered = jax.vmap(lambda table, picks: table[picks])(attention_in, where_rows)
    renewed = jnp.einsum('pkd,de->pke', gathered.astype(jnp.float32), keyval_weight.astype(jnp.float32)).astype(jnp.bfloat16)
    keyval = jax.vmap(lambda table, picks, newer: table.at[picks].set(newer))(cached_keyval, where_rows, renewed)
    queries = jnp.dot(attention_in, query_weight, preferred_element_type=jnp.float32).astype(jnp.bfloat16)
    segment_tag = (jnp.repeat(group_segments, 4, axis=1) + 1).astype(jnp.int32)
    zero_rows = jnp.zeros((NPACK, ROWS, 2 * D), jnp.bfloat16)
    padded_keyval = jnp.concatenate([zero_rows, keyval, zero_rows], axis=1)
    zero_tags = jnp.zeros((NPACK, ROWS), jnp.int32)
    padded_tag = jnp.concatenate([zero_tags, segment_tag, zero_tags], axis=1)
    context = lax.map(attend_pack, (queries, padded_keyval, padded_tag, segment_tag))
    stream = (stream_in + jnp.dot(context, output_weight, preferred_element_type=jnp.float32)).astype(jnp.bfloat16)
    projected = lax.map(make_tail(expand_weight, reduce_weight, merge_weight), stream)
    per_source = jnp.transpose(projected.reshape(NPACK, N_SEQ, MROWS, OUT), (1, 0, 2, 3)).reshape(N_SEQ, NPACK * MROWS, OUT)
    placed = jax.vmap(dispatch_rows)(per_source, owners)
    return jnp.transpose(placed, (1, 0, 2, 3))
```

```python
import math

import jax
import jax.numpy as jnp
from jax import lax
from jax.sharding import PartitionSpec as P

HEADS = 16
HEAD = 88
PAIR = 768
PICK = 32
F32 = jnp.float32
BF16 = jnp.bfloat16


def layer_norm(values):
    average = jnp.mean(values, axis=-1, keepdims=True)
    centered = values - average
    variance = jnp.mean(centered * centered, axis=-1, keepdims=True)
    return centered * lax.rsqrt(variance + 1e-06)


def swap(value):
    return lax.ppermute(value, "blk", [(b, b ^ 1) for b in range(8)])


def shift(value, steps):
    return lax.ppermute(value, "blk", [(b, (b + 2 * steps) % 8) for b in range(8)])


def neighbours(value):
    count = lax.axis_size("seq")
    up = [(i, i + 1) for i in range(count - 1)]
    before = lax.ppermute(value, "seq", up)
    after = lax.ppermute(value, "seq", [(j, i) for i, j in up])
    return before, after


def dot(a, b):
    return lax.dot_general(a, b, (((1,), (0,)), ((), ())), preferred_element_type=F32)


def dot_t(a, b):
    return lax.dot_general(a, b, (((1,), (1,)), ((), ())), preferred_element_type=F32)


def attend(queries, keyval, query_tag, key_tag):
    feature_count = queries.shape[1]
    query_heads = queries.reshape(queries.shape[0], HEADS, HEAD)
    key_rows = keyval[:, :feature_count].reshape(keyval.shape[0], HEADS, HEAD)
    value_rows = keyval[:, feature_count:].reshape(keyval.shape[0], HEADS, HEAD)
    scores = jnp.einsum(
        "qhd,khd->hqk", query_heads, key_rows, preferred_element_type=F32
    ) * (1.0 / math.sqrt(HEAD))
    allowed = query_tag[:, None] == key_tag[None, :]
    scores = jnp.where(allowed[None], scores, -1e30)
    highest = jnp.max(scores, axis=-1, keepdims=True)
    raised = jnp.exp(scores - highest)
    totals = jnp.sum(raised, axis=-1)
    weights = raised.astype(BF16)
    context = jnp.einsum("hqk,khd->qhd", weights, value_rows, preferred_element_type=F32)
    context = context / jnp.transpose(totals)[:, :, None]
    return context.reshape(queries.shape[0], feature_count).astype(BF16)


def feed(rows, expand_weight, reduce_weight):
    hidden = jax.nn.gelu(dot(rows, expand_weight), approximate=False).astype(BF16)
    return dot(hidden, reduce_weight)


def on_device(
    patches,
    group_segments,
    cached_keyval,
    recompute_rows,
    query_weight,
    keyval_weight,
    output_weight,
    expand_weight,
    reduce_weight,
    merge_weight,
    owners,
):
    rows = patches.shape[1]
    width = patches.shape[2]
    blk = lax.axis_index("blk")
    chip, core = blk // 2, blk % 2
    sources = lax.axis_size("seq")

    lane = core * (width - PAIR)
    keyval_slab = lax.dynamic_slice(keyval_weight.T, (0, lane), (keyval_weight.shape[1], PAIR))
    keyval_full = lax.all_gather(keyval_slab, "seq", axis=0, tiled=True)

    shard = query_weight.shape[1]
    quarter = shard // 4
    pieces = [
        lax.dynamic_slice(w, (chip * quarter, lane), (quarter, PAIR))
        for w in (query_weight.T, output_weight)
    ]
    piece = jnp.concatenate(pieces, axis=0)
    spread = jnp.broadcast_to(piece[None], (sources,) + piece.shape)
    spread = lax.all_to_all(spread, "seq", 0, 0, tiled=True)
    query_own = spread[:, :quarter].reshape(sources * quarter, PAIR)
    output_own = spread[:, quarter:].reshape(sources * quarter, PAIR)
    query_part = [query_own] + [shift(query_own, j) for j in (1, 3, 2)]
    query_part[3] , output_own = lax.optimization_barrier((query_part[3], output_own))
    output_part = [output_own] + [shift(output_own, j) for j in (1, 3, 2)]
    order = (0, 1, 3, 2)
    query_other = [swap(w) for w in query_part]
    output_other = [swap(w) for w in output_part]
    block = sources * quarter
    m = lax.broadcasted_iota(jnp.int32, (4 * block, width), 0)
    n = lax.broadcasted_iota(jnp.int32, (4 * block, width), 1)
    jm = m // block
    step = jnp.where(jm == 2, 3, jnp.where(jm == 3, 2, jm))
    natural = ((m % block) // quarter) * shard + ((chip - step + 4) % 4) * quarter + m % quarter
    reorder = (natural == n).astype(BF16)

    cached = cached_keyval[0]
    cached, _ = lax.optimization_barrier((cached, spread))
    cached_before, cached_after = neighbours(cached)
    segment_tag = jnp.repeat(group_segments[0], 4) + 1
    tag_before, tag_after = neighbours(segment_tag)

    stream_in = patches[0].astype(F32)
    attention_in = layer_norm(stream_in).astype(BF16)
    chosen = jnp.pad(recompute_rows[0, 0], (0, PICK - recompute_rows.shape[2]), constant_values=-1)
    row_of = lax.broadcasted_iota(jnp.int32, (PICK, rows), 1)
    chosen_rows = dot((chosen[:, None] == row_of).astype(BF16), attention_in).astype(BF16)
    chosen_before, chosen_after = neighbours(chosen)
    rows_before, rows_after = neighbours(chosen_rows)
    picked = jnp.concatenate([rows_before, chosen_rows, rows_after], axis=0)
    both = jnp.concatenate([picked, swap(picked)], axis=0)
    both = lax.dynamic_slice(both, (0, lane), (both.shape[0], PAIR))
    keep = (lax.broadcasted_iota(jnp.int32, both.shape, 1) >= core * (2 * PAIR - width)).astype(BF16)
    partial = dot_t(both * keep, keyval_full)
    renewed = (partial[: 3 * PICK] + swap(partial[3 * PICK :])).astype(BF16)

    def patched(old, index, fresh):
        hit = index[None, :] == lax.broadcasted_iota(jnp.int32, (rows, PICK), 0)
        new = dot(hit.astype(BF16), fresh).astype(BF16)
        return jnp.where(jnp.any(hit, axis=1, keepdims=True), new, old)

    keyval = jnp.concatenate(
        [
            patched(cached_before, chosen_before, renewed[:PICK]),
            patched(cached, chosen, renewed[PICK : 2 * PICK]),
            patched(cached_after, chosen_after, renewed[2 * PICK :]),
        ],
        axis=0,
    )
    key_tag = jnp.concatenate([tag_before, segment_tag, tag_after])

    other_lane = (width - PAIR) - lane
    in_own = lax.dynamic_slice(attention_in, (0, lane), (rows, PAIR))
    in_other = lax.dynamic_slice(attention_in, (0, other_lane), (rows, PAIR))
    column = lax.broadcasted_iota(jnp.int32, in_other.shape, 1) + other_lane
    shared = (column >= width - PAIR) & (column < PAIR)
    in_other = jnp.where(shared, jnp.zeros_like(in_other), in_other)
    queries = jnp.concatenate(
        [dot_t(in_own, a) + dot_t(in_other, b) for a, b in zip(query_part, query_other)], axis=1
    ).astype(BF16)
    queries = dot(queries, reorder).astype(BF16)

    context = attend(queries, keyval, segment_tag, key_tag)
    context = dot_t(context, reorder).astype(BF16)
    out_own = dot(context, jnp.concatenate(output_part, axis=0))
    out_other = dot(context, jnp.concatenate(output_other, axis=0))
    left = jnp.where(core == 0, out_own, out_other)
    right = jnp.where(core == 0, out_other, out_own)
    attended = jnp.concatenate([left, right[:, 2 * PAIR - width :]], axis=1)
    stream = (stream_in + attended).astype(BF16)

    normed = layer_norm(stream.astype(F32)).astype(BF16)
    arrived = {0: normed}
    for j in (1, 3, 2):
        arrived[j] = shift(normed, j)
    total = None
    back = []
    for j in order:
        mine = arrived[j]
        other = swap(mine)
        part_other = feed(other, expand_weight, reduce_weight).astype(BF16)
        from_other = swap(part_other)
        part = feed(mine, expand_weight, reduce_weight) + from_other.astype(F32)
        if j == 0:
            total = part.astype(BF16).astype(F32)
        else:
            back.append(shift(part.astype(BF16), 4 - j))
    for value in back:
        total = total + value.astype(F32)
    combined = stream.astype(F32) + total
    merged = layer_norm(combined).astype(BF16).reshape(rows // 4, 4 * width)

    destination = owners[0]
    count = destination.shape[0]
    capacity = 3 * count // sources
    same = destination[:, None] == destination[None, :]
    t = lax.broadcasted_iota(jnp.int32, (count, count), 0)
    u = lax.broadcasted_iota(jnp.int32, (count, count), 1)
    position = jnp.sum((same & (u < t)).astype(jnp.int32), axis=1)
    slot_index = (destination * capacity + position).reshape(8, count // 8)
    packs = jnp.stack(
        [2 * ((chip - j + 4) % 4) + c for j in order for c in (core, 1 - core)]
    )
    slot_index = jnp.sum(
        jnp.where(packs[:, None, None] == jnp.arange(8)[None, :, None], slot_index[None], 0), axis=1
    ).reshape(count)
    dispatch = (
        slot_index[None, :] == lax.broadcasted_iota(jnp.int32, (sources * capacity, count), 0)
    ).astype(BF16)

    gathered = {0: merged}
    for j in (1, 3, 2):
        gathered[j] = shift(merged, j)
    projected = []
    for j in order:
        pair = jnp.concatenate([gathered[j], swap(gathered[j])], axis=0)
        projected.append(dot(pair, merge_weight).astype(BF16))
    projected = jnp.concatenate(projected, axis=0)
    outgoing = dot(dispatch, projected).astype(BF16)
    outgoing = outgoing.reshape(sources, capacity, projected.shape[1])
    received = lax.all_to_all(outgoing, "seq", split_axis=0, concat_axis=0, tiled=True)
    return received[None]


def solution(mesh):
    return jax.shard_map(
        on_device,
        mesh=mesh,
        in_specs=(
            P("blk", "seq", None),
            P("blk", "seq"),
            P("blk", "seq", None),
            P("blk", "seq", None),
            P(None, "seq"),
            P(None, "seq"),
            P("seq", None),
            P(None, "blk"),
            P("blk", None),
            P(None, "blk"),
            P("seq", None),
        ),
        out_specs=P("seq", None, None, "blk"),
        check_vma=False,
    )
```

```python
import math

import jax
import jax.numpy as jnp
from jax import lax
from jax.experimental import pallas as pl
from jax.experimental.pallas import tpu as pltpu
from jax.sharding import PartitionSpec as P

HEADS = 16
HEAD = 88
PAIR = 768
PICK = 32
F32 = jnp.float32
BF16 = jnp.bfloat16
VM = pltpu.VMEM


def layer_norm(values):
    average = jnp.mean(values, axis=-1, keepdims=True)
    centered = values - average
    variance = jnp.mean(centered * centered, axis=-1, keepdims=True)
    return centered * lax.rsqrt(variance + 1e-06)


def swap(value):
    return lax.ppermute(value, "blk", [(b, b ^ 1) for b in range(8)])


def shift(value, steps):
    return lax.ppermute(value, "blk", [(b, (b + 2 * steps) % 8) for b in range(8)])


def neighbours(value):
    count = lax.axis_size("seq")
    up = [(i, i + 1) for i in range(count - 1)]
    before = lax.ppermute(value, "seq", up)
    after = lax.ppermute(value, "seq", [(j, i) for i, j in up])
    return before, after


def dot(a, b):
    return lax.dot_general(a, b, (((1,), (0,)), ((), ())), preferred_element_type=F32)


def dot_t(a, b):
    return lax.dot_general(a, b, (((1,), (1,)), ((), ())), preferred_element_type=F32)


def after(*values):
    return lax.optimization_barrier(values)


def around(value):
    half = value.shape[0] // 2
    behind, ahead = shift(value, 1), shift(value, 3)
    opposite = jnp.concatenate([shift(behind[:half], 1), shift(ahead[half:], 3)], axis=0)
    return [value, behind, ahead, opposite]


def feed_kernel(*refs):
    if len(refs) == 5:
        x_ref, e_ref, r_ref, add_ref, o_ref = refs
    else:
        x_ref, e_ref, r_ref, o_ref = refs
        add_ref = None
    units = e_ref.shape[1]
    x = x_ref[...]
    total = None
    for k in range(0, units, 256):
        inner = jnp.dot(x, e_ref[:, k:k+256], preferred_element_type=F32)
        hidden = (0.5 * inner * (1.0 + lax.erf(inner * math.sqrt(0.5)))).astype(BF16)
        part = jnp.dot(hidden, r_ref[k:k+256, :], preferred_element_type=F32)
        total = part if total is None else total + part
    if add_ref is not None:
        total = total + add_ref[...].astype(F32)
    o_ref[...] = total.astype(BF16)


def feed(x, e, r, add=None):
    args = (x, e, r) + (() if add is None else (add,))
    return pl.pallas_call(
        feed_kernel,
        out_shape=jax.ShapeDtypeStruct((x.shape[0], r.shape[1]), BF16),
        in_specs=[pl.BlockSpec(memory_space=VM)] * len(args),
        out_specs=pl.BlockSpec(memory_space=VM),
        compiler_params=pltpu.CompilerParams(vmem_limit_bytes=40 << 20),
    )(*args)


def attend_kernel(q_ref, before_ref, own_ref, after_ref, fresh_ref, index_ref, qtag_ref, ktag_ref, o_ref, kv_ref, acc_ref):
    rows, width = q_ref.shape
    for b, old in enumerate((before_ref, own_ref, after_ref)):
        at = lax.broadcasted_iota(jnp.int32, (rows, PICK), 0)
        hit = (index_ref[b:b+1, :] == at).astype(F32)
        any_hit = jnp.max(hit, axis=1, keepdims=True) > 0.0
        hit = hit.astype(BF16)
        for k in range(0, 2*width, 256):
            new = jnp.dot(hit, fresh_ref[b*PICK:(b+1)*PICK, k:k+256], preferred_element_type=F32)
            kv_ref[b*rows:(b+1)*rows, k:k+256] = jnp.where(any_hit, new, old[:, k:k+256].astype(F32)).astype(BF16)
    allowed = qtag_ref[...] == ktag_ref[...]
    scale = 1.0 / math.sqrt(HEAD)
    for h in range(HEADS):
        lo = (HEAD*h)//128*128
        hi = -(-(HEAD*(h+1))//128)*128
        lane = lax.broadcasted_iota(jnp.int32, (rows, hi-lo), 1) + lo
        mine = (lane >= HEAD*h) & (lane < HEAD*(h+1))
        q = q_ref[:, lo:hi]
        q = jnp.where(mine, q.astype(F32), 0.0).astype(BF16)
        s = lax.dot_general(q, kv_ref[:, lo:hi], (((1,),(1,)),((),())), preferred_element_type=F32)
        s = jnp.where(allowed, s, -1e30)
        top = jnp.max(s, axis=1, keepdims=True)
        raised = jnp.exp((s - top) * scale)
        total = jnp.sum(raised, axis=1, keepdims=True)
        o = jnp.dot(raised.astype(BF16), kv_ref[:, width+lo:width+hi], preferred_element_type=F32)
        o = o / total
        acc_ref[:, lo:hi] = jnp.where(mine, o, acc_ref[:, lo:hi])
    o_ref[...] = acc_ref[...].astype(BF16)


def attend(q, before, own, after, fresh, index, qtag, ktag):
    rows, width = q.shape
    return pl.pallas_call(
        attend_kernel,
        out_shape=jax.ShapeDtypeStruct((rows, width), BF16),
        in_specs=[pl.BlockSpec(memory_space=VM)] * 8,
        out_specs=pl.BlockSpec(memory_space=VM),
        scratch_shapes=[VM((3*rows, 2*width), BF16), VM((rows, width), F32)],
        compiler_params=pltpu.CompilerParams(vmem_limit_bytes=40 << 20),
    )(q, before, own, after, fresh, index, qtag, ktag)


def on_device(
    patches,
    group_segments,
    cached_keyval,
    recompute_rows,
    query_weight,
    keyval_weight,
    output_weight,
    expand_weight,
    reduce_weight,
    merge_weight,
    owners,
):
    rows = patches.shape[1]
    width = patches.shape[2]
    blk = lax.axis_index("blk")
    chip, core = blk // 2, blk % 2
    sources = lax.axis_size("seq")

    lane = core * (width - PAIR)
    keyval_slab = lax.dynamic_slice(keyval_weight.T, (0, lane), (keyval_weight.shape[1], PAIR))
    keyval_slab, patches, query_weight, output_weight, group_segments, recompute_rows, owners = after(
        keyval_slab, patches, query_weight, output_weight, group_segments, recompute_rows, owners
    )
    keyval_full = lax.all_gather(keyval_slab, "seq", axis=0, tiled=True)

    shard = query_weight.shape[1]
    quarter = shard // 4
    pieces = [
        lax.dynamic_slice(w, (chip * quarter, lane), (quarter, PAIR))
        for w in (query_weight.T, output_weight)
    ]
    piece = jnp.concatenate(pieces, axis=0)
    spread = jnp.broadcast_to(piece[None], (sources,) + piece.shape)
    spread = lax.all_to_all(spread, "seq", 0, 0, tiled=True)
    query_own = spread[:, :quarter].reshape(sources * quarter, PAIR)
    output_own = spread[:, quarter:].reshape(sources * quarter, PAIR)
    query_part = around(query_own)
    output_own, query_part[1], query_part[2] = after(output_own, query_part[1], query_part[2])
    output_part = around(output_own)
    query_other = [swap(w) for w in query_part]
    output_other = [swap(w) for w in output_part]
    block = sources * quarter
    m = lax.broadcasted_iota(jnp.int32, (4 * block, width), 0)
    n = lax.broadcasted_iota(jnp.int32, (4 * block, width), 1)
    jm = m // block
    step = jnp.where(jm == 2, 3, jnp.where(jm == 3, 2, jm))
    natural = ((m % block) // quarter) * shard + ((chip - step + 4) % 4) * quarter + m % quarter
    reorder = (natural == n).astype(BF16)

    stream_in = patches[0].astype(F32)
    attention_in = layer_norm(stream_in).astype(BF16)
    picks = recompute_rows.shape[2]
    chosen = jnp.pad(recompute_rows[0, 0], (0, PICK - picks), constant_values=-1)
    row_of = lax.broadcasted_iota(jnp.int32, (PICK, rows), 1)
    chosen_rows = dot((chosen[:, None] == row_of).astype(BF16), attention_in).astype(BF16)
    segment_tag = jnp.repeat(group_segments[0], 4) + 1
    lines = rows // 128
    extra = jnp.concatenate(
        [
            jnp.pad(chosen[: PICK - lines, None].astype(BF16), ((0, 0), (0, 127))),
            segment_tag.astype(BF16).reshape(lines, 128),
        ],
        axis=0,
    )
    packet = jnp.concatenate([chosen_rows, extra], axis=1)
    packet_before, packet_after = neighbours(packet)

    def unpack(value):
        index = value[: PICK - lines, width].astype(jnp.int32)
        index = jnp.pad(index, (0, lines), constant_values=-1)
        return index, value[PICK - lines :, width:].reshape(rows).astype(jnp.int32)

    index_before, tag_before = unpack(packet_before)
    index_after, tag_after = unpack(packet_after)
    index = jnp.stack([index_before, chosen, index_after])
    key_tag = jnp.concatenate([tag_before, segment_tag, tag_after])

    cached = cached_keyval[0]
    cached, spread, packet_before = after(cached, spread, packet_before)
    cached_before, cached_after = neighbours(cached)

    other_lane = (width - PAIR) - lane
    in_own = lax.dynamic_slice(attention_in, (0, lane), (rows, PAIR))
    in_other = lax.dynamic_slice(attention_in, (0, other_lane), (rows, PAIR))
    column = lax.broadcasted_iota(jnp.int32, in_other.shape, 1) + other_lane
    shared = (column >= width - PAIR) & (column < PAIR)
    in_other = jnp.where(shared, jnp.zeros_like(in_other), in_other)
    queries = jnp.concatenate(
        [dot_t(in_own, a) + dot_t(in_other, b) for a, b in zip(query_part, query_other)], axis=1
    ).astype(BF16)
    queries = dot(queries, reorder).astype(BF16)

    picked = jnp.concatenate([packet_before, packet, packet_after], axis=0)[:, :width]
    both = jnp.concatenate([picked, swap(picked)], axis=0)
    both = lax.dynamic_slice(both, (0, lane), (both.shape[0], PAIR))
    keep = (lax.broadcasted_iota(jnp.int32, both.shape, 1) >= core * (2 * PAIR - width)).astype(BF16)
    both, queries = after(both * keep, queries)
    partial = dot_t(both, keyval_full)
    renewed = (partial[: 3 * PICK] + swap(partial[3 * PICK :])).astype(BF16)

    context = attend(
        queries, cached_before, cached, cached_after, renewed, index, segment_tag[:, None], key_tag[None]
    )
    context = dot_t(context, reorder).astype(BF16)
    out_own = dot(context, jnp.concatenate(output_part, axis=0))
    out_other = dot(context, jnp.concatenate(output_other, axis=0))
    left = jnp.where(core == 0, out_own, out_other)
    right = jnp.where(core == 0, out_other, out_own)
    attended = jnp.concatenate([left, right[:, 2 * PAIR - width :]], axis=1)
    stream = (stream_in + attended).astype(BF16)

    normed = layer_norm(stream.astype(F32)).astype(BF16)
    mine = around(normed)
    weights = (expand_weight, reduce_weight)

    def other_part(value):
        return swap(feed(value, *weights))

    def chip_part(value, from_other):
        return feed(value, *weights, from_other)

    from_0 = other_part(swap(mine[0]))
    part_0 = chip_part(mine[0], from_0)
    mine[1], mine[2], part_0 = after(mine[1], mine[2], part_0)
    other_1, other_2 = swap(mine[1]), swap(mine[2])
    from_1 = other_part(other_1)
    from_2 = other_part(other_2)
    part_1 = chip_part(mine[1], from_1)
    back_1 = shift(part_1, 3)
    part_2 = chip_part(mine[2], from_2)
    back_2 = shift(part_2, 1)
    mine[3], part_1 = after(mine[3], part_1)
    from_3 = other_part(swap(mine[3]))
    back_3 = shift(chip_part(mine[3], from_3), 2)
    total = part_0.astype(F32) + back_1.astype(F32) + back_2.astype(F32) + back_3.astype(F32)
    combined = stream.astype(F32) + total
    merged = layer_norm(combined).astype(BF16).reshape(rows // 4, 4 * width)

    destination = owners[0]
    count = destination.shape[0]
    capacity = 3 * count // sources
    same = destination[:, None] == destination[None, :]
    t = lax.broadcasted_iota(jnp.int32, (count, count), 0)
    u = lax.broadcasted_iota(jnp.int32, (count, count), 1)
    position = jnp.sum((same & (u < t)).astype(jnp.int32), axis=1)
    slot_index = (destination * capacity + position).reshape(8, count // 8)
    packs = jnp.stack(
        [2 * ((chip - j + 4) % 4) + c for j in (0, 1, 3, 2) for c in (core, 1 - core)]
    )
    slot_index = jnp.sum(
        jnp.where(packs[:, None, None] == jnp.arange(8)[None, :, None], slot_index[None], 0), axis=1
    ).reshape(count)
    dispatch = (
        slot_index[None, :] == lax.broadcasted_iota(jnp.int32, (sources * capacity, count), 0)
    ).astype(BF16)
    dispatch, merged = after(dispatch, merged)

    projected = []
    for value in around(merged):
        pair = jnp.concatenate([value, swap(value)], axis=0)
        projected.append(dot(pair, merge_weight).astype(BF16))
    projected = jnp.concatenate(projected, axis=0)
    outgoing = dot(dispatch, projected).astype(BF16)
    outgoing = outgoing.reshape(sources, capacity, projected.shape[1])
    received = lax.all_to_all(outgoing, "seq", split_axis=0, concat_axis=0, tiled=True)
    return received[None]


def solution(mesh):
    return jax.shard_map(
        on_device,
        mesh=mesh,
        in_specs=(
            P("blk", "seq", None),
            P("blk", "seq"),
            P("blk", "seq", None),
            P("blk", "seq", None),
            P(None, "seq"),
            P(None, "seq"),
            P("seq", None),
            P(None, "blk"),
            P("blk", None),
            P(None, "blk"),
            P("seq", None),
        ),
        out_specs=P("seq", None, None, "blk"),
        check_vma=False,
    )
```

```python
import math

import jax
import jax.numpy as jnp
from jax import lax
from jax.experimental import pallas as pl
from jax.experimental.pallas import tpu as pltpu
from jax.sharding import PartitionSpec as P

HEADS = 16
HEAD = 88
PAIR = 768
PICK = 32
F32 = jnp.float32
BF16 = jnp.bfloat16
VM = pltpu.VMEM
ORDER = (0, 1, 3, 2)


def layer_norm(values):
    average = jnp.mean(values, axis=-1, keepdims=True)
    centered = values - average
    variance = jnp.mean(centered * centered, axis=-1, keepdims=True)
    return centered * lax.rsqrt(variance + 1e-06)


def swap(value):
    return lax.ppermute(value, "blk", [(b, b ^ 1) for b in range(8)])


def shift(value, steps):
    return lax.ppermute(value, "blk", [(b, (b + 2 * steps) % 8) for b in range(8)])


def neighbours(value):
    count = lax.axis_size("seq")
    up = [(i, i + 1) for i in range(count - 1)]
    before = lax.ppermute(value, "seq", up)
    after = lax.ppermute(value, "seq", [(j, i) for i, j in up])
    return before, after


def dot(a, b):
    return lax.dot_general(a, b, (((1,), (0,)), ((), ())), preferred_element_type=F32)


def dot_t(a, b):
    return lax.dot_general(a, b, (((1,), (1,)), ((), ())), preferred_element_type=F32)


def after(*values):
    return lax.optimization_barrier(values)


def shift_y(value, steps):
    count = lax.axis_size("seq")
    return lax.ppermute(value, "seq", [(s, (s + 8 * steps) % count) for s in range(count)])


def around(value, shift):
    half = value.shape[0] // 2
    behind, ahead = shift(value, 1), shift(value, 3)
    opposite = jnp.concatenate([shift(behind[:half], 1), shift(ahead[half:], 3)], axis=0)
    return [value, behind, ahead, opposite]


def feed_kernel(*refs):
    if len(refs) == 5:
        x_ref, e_ref, r_ref, add_ref, o_ref = refs
    else:
        x_ref, e_ref, r_ref, o_ref = refs
        add_ref = None
    units = e_ref.shape[1]
    x = x_ref[...]
    total = None
    for k in range(0, units, 256):
        inner = jnp.dot(x, e_ref[:, k:k+256], preferred_element_type=F32)
        hidden = (0.5 * inner * (1.0 + lax.erf(inner * math.sqrt(0.5)))).astype(BF16)
        part = jnp.dot(hidden, r_ref[k:k+256, :], preferred_element_type=F32)
        total = part if total is None else total + part
    if add_ref is not None:
        total = total + add_ref[...].astype(F32)
    o_ref[...] = total.astype(BF16)


def feed(x, e, r, add=None):
    args = (x, e, r) + (() if add is None else (add,))
    return pl.pallas_call(
        feed_kernel,
        out_shape=jax.ShapeDtypeStruct((x.shape[0], r.shape[1]), BF16),
        in_specs=[pl.BlockSpec(memory_space=VM)] * len(args),
        out_specs=pl.BlockSpec(memory_space=VM),
        compiler_params=pltpu.CompilerParams(vmem_limit_bytes=40 << 20),
    )(*args)


def attend_kernel(q_ref, before_ref, own_ref, after_ref, fresh_ref, index_ref, qtag_ref, ktag_ref, o_ref, kv_ref, acc_ref):
    rows, width = q_ref.shape
    for b, old in enumerate((before_ref, own_ref, after_ref)):
        at = lax.broadcasted_iota(jnp.int32, (rows, PICK), 0)
        hit = (index_ref[b:b+1, :] == at).astype(F32)
        any_hit = jnp.max(hit, axis=1, keepdims=True) > 0.0
        hit = hit.astype(BF16)
        for k in range(0, 2*width, 256):
            new = jnp.dot(hit, fresh_ref[b*PICK:(b+1)*PICK, k:k+256], preferred_element_type=F32)
            kv_ref[b*rows:(b+1)*rows, k:k+256] = jnp.where(any_hit, new, old[:, k:k+256].astype(F32)).astype(BF16)
    allowed = qtag_ref[...] == ktag_ref[...]
    scale = 1.0 / math.sqrt(HEAD)
    for h in range(HEADS):
        lo = (HEAD*h)//128*128
        hi = -(-(HEAD*(h+1))//128)*128
        lane = lax.broadcasted_iota(jnp.int32, (rows, hi-lo), 1) + lo
        mine = (lane >= HEAD*h) & (lane < HEAD*(h+1))
        q = q_ref[:, lo:hi]
        q = jnp.where(mine, q.astype(F32), 0.0).astype(BF16)
        s = lax.dot_general(q, kv_ref[:, lo:hi], (((1,),(1,)),((),())), preferred_element_type=F32)
        s = jnp.where(allowed, s, -1e30)
        top = jnp.max(s, axis=1, keepdims=True)
        raised = jnp.exp((s - top) * scale)
        total = jnp.sum(raised, axis=1, keepdims=True)
        o = jnp.dot(raised.astype(BF16), kv_ref[:, width+lo:width+hi], preferred_element_type=F32)
        o = o / total
        acc_ref[:, lo:hi] = jnp.where(mine, o, acc_ref[:, lo:hi])
    o_ref[...] = acc_ref[...].astype(BF16)


def attend(q, before, own, after, fresh, index, qtag, ktag):
    rows, width = q.shape
    return pl.pallas_call(
        attend_kernel,
        out_shape=jax.ShapeDtypeStruct((rows, width), BF16),
        in_specs=[pl.BlockSpec(memory_space=VM)] * 8,
        out_specs=pl.BlockSpec(memory_space=VM),
        scratch_shapes=[VM((3*rows, 2*width), BF16), VM((rows, width), F32)],
        compiler_params=pltpu.CompilerParams(vmem_limit_bytes=40 << 20),
    )(q, before, own, after, fresh, index, qtag, ktag)


def on_device(
    patches,
    group_segments,
    cached_keyval,
    recompute_rows,
    query_weight,
    keyval_weight,
    output_weight,
    expand_weight,
    reduce_weight,
    merge_weight,
    owners,
):
    rows = patches.shape[1]
    width = patches.shape[2]
    blk = lax.axis_index("blk")
    chip, core = blk // 2, blk % 2
    sources = lax.axis_size("seq")

    lane = core * (width - PAIR)
    shard = query_weight.shape[1]
    quarter = shard // 4
    pair = keyval_weight.shape[1]

    def half(weight, start, count):
        return lax.dynamic_slice(weight, (start, lane), (count, PAIR))

    piece = jnp.concatenate(
        [
            half(keyval_weight.T, 0, pair),
            half(query_weight.T, chip * quarter, quarter),
            half(output_weight, chip * quarter, quarter),
        ],
        axis=0,
    )
    depth, height = 8, sources // 8
    groups = [[y * depth + z for z in range(depth)] for y in range(height)]
    spread = jnp.broadcast_to(piece[None], (depth,) + piece.shape)
    spread, patches, recompute_rows = after(spread, patches, recompute_rows)
    spread = lax.all_to_all(spread, "seq", 0, 0, axis_index_groups=groups, tiled=True)
    keyval_own = spread[:, :pair].reshape(depth * pair, PAIR)
    slim = depth * quarter
    small = jnp.concatenate(
        [
            spread[:, pair : pair + quarter].reshape(slim, PAIR),
            spread[:, pair + quarter :].reshape(slim, PAIR),
        ],
        axis=0,
    )
    column = lax.axis_index("seq") // depth
    small = around(small, shift_y)
    keyval_parts = around(keyval_own, shift_y)
    query_own = jnp.concatenate([v[:slim] for v in small], axis=0)
    output_own = jnp.concatenate([v[slim:] for v in small], axis=0)
    query_part = around(query_own, shift)
    output_own, query_part[1], query_part[2] = after(output_own, query_part[1], query_part[2])
    output_part = around(output_own, shift)
    m = lax.broadcasted_iota(jnp.int32, (width, width), 0)
    n = lax.broadcasted_iota(jnp.int32, (width, width), 1)

    def steps_of(place):
        return jnp.where(place == 2, 3, jnp.where(place == 3, 2, place))

    block = height * slim
    source_chip = (chip - steps_of(m // block) + 4) % 4
    source_column = (column - steps_of((m % block) // slim) + height) % height
    source = source_column * depth + (m % slim) // quarter
    natural = source * shard + source_chip * quarter + m % quarter
    reorder = (natural == n).astype(BF16)

    stream_in = patches[0].astype(F32)
    attention_in = layer_norm(stream_in).astype(BF16)
    picks = recompute_rows.shape[2]
    chosen = jnp.pad(recompute_rows[0, 0], (0, PICK - picks), constant_values=-1)
    row_of = lax.broadcasted_iota(jnp.int32, (PICK, rows), 1)
    chosen_rows = dot((chosen[:, None] == row_of).astype(BF16), attention_in).astype(BF16)
    segment_tag = jnp.repeat(group_segments[0], 4) + 1
    lines = rows // 128
    extra = jnp.concatenate(
        [
            jnp.pad(chosen[: PICK - lines, None].astype(BF16), ((0, 0), (0, 127))),
            segment_tag.astype(BF16).reshape(lines, 128),
        ],
        axis=0,
    )
    packet = jnp.concatenate([chosen_rows, extra], axis=1)
    packet_before, packet_after = neighbours(packet)

    def unpack(value):
        index = value[: PICK - lines, width].astype(jnp.int32)
        index = jnp.pad(index, (0, lines), constant_values=-1)
        return index, value[PICK - lines :, width:].reshape(rows).astype(jnp.int32)

    index_before, tag_before = unpack(packet_before)
    index_after, tag_after = unpack(packet_after)
    index = jnp.stack([index_before, chosen, index_after])
    key_tag = jnp.concatenate([tag_before, segment_tag, tag_after])

    cached = cached_keyval[0]
    cached, spread, packet_before = after(cached, spread, packet_before)
    cached_before, cached_after = neighbours(cached)

    query_other = [swap(w) for w in query_part]
    query_part[1], query_part[2], near_1, near_2 = after(
        query_part[1], query_part[2], keyval_parts[1], keyval_parts[2]
    )
    query_part[3], cached_before, cached_after = after(query_part[3], cached_before, cached_after)
    keyval_full = jnp.zeros((sources * pair, PAIR), BF16)
    for steps, part in zip(ORDER, (keyval_own, near_1, near_2, keyval_parts[3])):
        place = ((column - steps + height) % height) * depth * pair
        keyval_full = lax.dynamic_update_slice(keyval_full, part, (place, 0))
    output_other = [swap(w) for w in output_part]

    other_lane = (width - PAIR) - lane
    in_own = lax.dynamic_slice(attention_in, (0, lane), (rows, PAIR))
    in_other = lax.dynamic_slice(attention_in, (0, other_lane), (rows, PAIR))
    at = lax.broadcasted_iota(jnp.int32, in_other.shape, 1) + other_lane
    shared = (at >= width - PAIR) & (at < PAIR)
    in_other = jnp.where(shared, jnp.zeros_like(in_other), in_other)
    queries = jnp.concatenate(
        [dot_t(in_own, a) + dot_t(in_other, b) for a, b in zip(query_part, query_other)], axis=1
    ).astype(BF16)
    queries = dot(queries, reorder).astype(BF16)

    picked = jnp.concatenate([packet_before, packet, packet_after], axis=0)[:, :width]
    both = jnp.concatenate([picked, swap(picked)], axis=0)
    both = lax.dynamic_slice(both, (0, lane), (both.shape[0], PAIR))
    keep = (lax.broadcasted_iota(jnp.int32, both.shape, 1) >= core * (2 * PAIR - width)).astype(BF16)
    both, queries = after(both * keep, queries)
    partial = dot_t(both, keyval_full)
    renewed = (partial[: 3 * PICK] + swap(partial[3 * PICK :])).astype(BF16)

    context = attend(
        queries, cached_before, cached, cached_after, renewed, index, segment_tag[:, None], key_tag[None]
    )
    context = dot_t(context, reorder).astype(BF16)
    out_own = dot(context, jnp.concatenate(output_part, axis=0))
    out_other = dot(context, jnp.concatenate(output_other, axis=0))
    left = jnp.where(core == 0, out_own, out_other)
    right = jnp.where(core == 0, out_other, out_own)
    attended = jnp.concatenate([left, right[:, 2 * PAIR - width :]], axis=1)
    stream = (stream_in + attended).astype(BF16)

    normed = layer_norm(stream.astype(F32)).astype(BF16)
    behind, ahead = shift(normed, 1), shift(normed, 3)
    weights = (expand_weight, reduce_weight)

    def other_part(value):
        return swap(feed(value, *weights))

    def chip_part(value, from_other):
        return feed(value, *weights, from_other)

    part_0 = chip_part(normed, other_part(swap(normed)))
    behind, ahead, part_0 = after(behind, ahead, part_0)
    top, bottom = shift(behind[: rows // 2], 1), shift(ahead[rows // 2 :], 3)
    other_1, other_2 = swap(behind), swap(ahead)
    from_1 = other_part(other_1)
    from_2 = other_part(other_2)
    part_1 = chip_part(behind, from_1)
    back_1 = shift(part_1, 3)
    part_2 = chip_part(ahead, from_2)
    back_2 = shift(part_2, 1)
    top, bottom, part_1, part_2 = after(top, bottom, part_1, part_2)
    opposite = jnp.concatenate([top, bottom], axis=0)
    from_3 = other_part(swap(opposite))
    back_3 = shift(chip_part(opposite, from_3), 2)
    total = part_0.astype(F32) + back_1.astype(F32) + back_2.astype(F32) + back_3.astype(F32)
    combined = stream.astype(F32) + total
    merged = layer_norm(combined).astype(BF16).reshape(rows // 4, 4 * width)

    destination = owners[0]
    count = destination.shape[0]
    capacity = 3 * count // sources
    same = destination[:, None] == destination[None, :]
    t = lax.broadcasted_iota(jnp.int32, (count, count), 0)
    u = lax.broadcasted_iota(jnp.int32, (count, count), 1)
    position = jnp.sum((same & (u < t)).astype(jnp.int32), axis=1)
    slot_index = (destination * capacity + position).reshape(8, count // 8)
    packs = jnp.stack(
        [2 * ((chip - j + 4) % 4) + c for j in ORDER for c in (core, 1 - core)]
    )
    slot_index = jnp.sum(
        jnp.where(packs[:, None, None] == jnp.arange(8)[None, :, None], slot_index[None], 0), axis=1
    ).reshape(count)
    dispatch = (
        slot_index[None, :] == lax.broadcasted_iota(jnp.int32, (sources * capacity, count), 0)
    ).astype(BF16)
    dispatch, merged = after(dispatch, merged)

    projected = []
    for value in around(merged, shift):
        pair = jnp.concatenate([value, swap(value)], axis=0)
        projected.append(dot(pair, merge_weight).astype(BF16))
    projected = jnp.concatenate(projected, axis=0)
    outgoing = dot(dispatch, projected).astype(BF16)
    outgoing = outgoing.reshape(sources, capacity, projected.shape[1])
    received = lax.all_to_all(outgoing, "seq", split_axis=0, concat_axis=0, tiled=True)
    return received[None]


def solution(mesh):
    return jax.shard_map(
        on_device,
        mesh=mesh,
        in_specs=(
            P("blk", "seq", None),
            P("blk", "seq"),
            P("blk", "seq", None),
            P("blk", "seq", None),
            P(None, "seq"),
            P(None, "seq"),
            P("seq", None),
            P(None, "blk"),
            P("blk", None),
            P(None, "blk"),
            P("seq", None),
        ),
        out_specs=P("seq", None, None, "blk"),
        check_vma=False,
    )
```

```python
import math

import jax
import jax.numpy as jnp
from jax import lax
from jax.experimental import pallas as pl
from jax.experimental.pallas import tpu as pltpu
from jax.sharding import PartitionSpec as P

HEADS = 16
HEAD = 88
PAIR = 768
PICK = 32
F32 = jnp.float32
BF16 = jnp.bfloat16
VM = pltpu.VMEM
ORDER = (0, 1, 3, 2)


def layer_norm(values):
    average = jnp.mean(values, axis=-1, keepdims=True)
    centered = values - average
    variance = jnp.mean(centered * centered, axis=-1, keepdims=True)
    return centered * lax.rsqrt(variance + 1e-06)


def swap(value):
    return lax.ppermute(value, "blk", [(b, b ^ 1) for b in range(8)])


def shift(value, steps):
    return lax.ppermute(value, "blk", [(b, (b + 2 * steps) % 8) for b in range(8)])


def neighbours(value):
    count = lax.axis_size("seq")
    up = [(i, i + 1) for i in range(count - 1)]
    before = lax.ppermute(value, "seq", up)
    after = lax.ppermute(value, "seq", [(j, i) for i, j in up])
    return before, after


def dot(a, b):
    return lax.dot_general(a, b, (((1,), (0,)), ((), ())), preferred_element_type=F32)


def dot_t(a, b):
    return lax.dot_general(a, b, (((1,), (1,)), ((), ())), preferred_element_type=F32)


def after(*values):
    return lax.optimization_barrier(values)


def shift_y(value, steps):
    count = lax.axis_size("seq")
    return lax.ppermute(value, "seq", [(s, (s + 8 * steps) % count) for s in range(count)])


def around(value, shift):
    behind, ahead = shift(value, 1), shift(value, 3)
    return [value, behind, ahead, across(behind, ahead, shift)]


def across(behind, ahead, shift):
    middle = behind.shape[0] // 2
    return jnp.concatenate([shift(behind[:middle], 1), shift(ahead[middle:], 3)], axis=0)


def feed_kernel(*refs):
    if len(refs) == 5:
        x_ref, e_ref, r_ref, add_ref, o_ref = refs
    else:
        x_ref, e_ref, r_ref, o_ref = refs
        add_ref = None
    units = e_ref.shape[1]
    x = x_ref[...]
    total = None
    for k in range(0, units, 256):
        inner = jnp.dot(x, e_ref[:, k:k+256], preferred_element_type=F32)
        hidden = (0.5 * inner * (1.0 + lax.erf(inner * math.sqrt(0.5)))).astype(BF16)
        part = jnp.dot(hidden, r_ref[k:k+256, :], preferred_element_type=F32)
        total = part if total is None else total + part
    if add_ref is not None:
        total = total + add_ref[...].astype(F32)
    o_ref[...] = total.astype(BF16)


def feed(x, e, r, add=None):
    args = (x, e, r) + (() if add is None else (add,))
    return pl.pallas_call(
        feed_kernel,
        out_shape=jax.ShapeDtypeStruct((x.shape[0], r.shape[1]), BF16),
        in_specs=[pl.BlockSpec(memory_space=VM)] * len(args),
        out_specs=pl.BlockSpec(memory_space=VM),
        compiler_params=pltpu.CompilerParams(vmem_limit_bytes=40 << 20),
        cost_estimate=pl.CostEstimate(
            flops=4 * x.shape[0] * e.shape[0] * e.shape[1],
            transcendentals=x.shape[0] * e.shape[1],
            bytes_accessed=2 * (2 * x.size + e.size + r.size),
        ),
    )(*args)


def attend_kernel(q_ref, before_ref, own_ref, after_ref, fresh_ref, index_ref, qtag_ref, ktag_ref, o_ref, kv_ref, acc_ref):
    rows, width = q_ref.shape
    for b, old in enumerate((before_ref, own_ref, after_ref)):
        at = lax.broadcasted_iota(jnp.int32, (rows, PICK), 0)
        hit = (index_ref[b:b+1, :] == at).astype(F32)
        any_hit = jnp.max(hit, axis=1, keepdims=True) > 0.0
        hit = hit.astype(BF16)
        for k in range(0, 2*width, 256):
            new = jnp.dot(hit, fresh_ref[b*PICK:(b+1)*PICK, k:k+256], preferred_element_type=F32)
            kv_ref[b*rows:(b+1)*rows, k:k+256] = jnp.where(any_hit, new, old[:, k:k+256].astype(F32)).astype(BF16)
    allowed = qtag_ref[...] == ktag_ref[...]
    scale = 1.0 / math.sqrt(HEAD)
    for h in range(HEADS):
        lo = (HEAD*h)//128*128
        hi = -(-(HEAD*(h+1))//128)*128
        lane = lax.broadcasted_iota(jnp.int32, (rows, hi-lo), 1) + lo
        mine = (lane >= HEAD*h) & (lane < HEAD*(h+1))
        q = q_ref[:, lo:hi]
        q = jnp.where(mine, q.astype(F32), 0.0).astype(BF16)
        s = lax.dot_general(q, kv_ref[:, lo:hi], (((1,),(1,)),((),())), preferred_element_type=F32)
        s = jnp.where(allowed, s, -1e30)
        top = jnp.max(s, axis=1, keepdims=True)
        raised = jnp.exp((s - top) * scale)
        total = jnp.sum(raised, axis=1, keepdims=True)
        o = jnp.dot(raised.astype(BF16), kv_ref[:, width+lo:width+hi], preferred_element_type=F32)
        o = o / total
        acc_ref[:, lo:hi] = jnp.where(mine, o, acc_ref[:, lo:hi])
    o_ref[...] = acc_ref[...].astype(BF16)


def attend(q, before, own, after, fresh, index, qtag, ktag):
    rows, width = q.shape
    return pl.pallas_call(
        attend_kernel,
        out_shape=jax.ShapeDtypeStruct((rows, width), BF16),
        in_specs=[pl.BlockSpec(memory_space=VM)] * 8,
        out_specs=pl.BlockSpec(memory_space=VM),
        scratch_shapes=[VM((3*rows, 2*width), BF16), VM((rows, width), F32)],
        compiler_params=pltpu.CompilerParams(vmem_limit_bytes=40 << 20),
        cost_estimate=pl.CostEstimate(
            flops=12 * rows * rows * width,
            transcendentals=3 * HEADS * rows * rows,
            bytes_accessed=2 * (2 * q.size + 3 * own.size),
        ),
    )(q, before, own, after, fresh, index, qtag, ktag)


def on_device(
    patches,
    group_segments,
    cached_keyval,
    recompute_rows,
    query_weight,
    keyval_weight,
    output_weight,
    expand_weight,
    reduce_weight,
    merge_weight,
    owners,
):
    rows = patches.shape[1]
    width = patches.shape[2]
    blk = lax.axis_index("blk")
    chip, core = blk // 2, blk % 2
    sources = lax.axis_size("seq")

    lane = core * (width - PAIR)
    shard = query_weight.shape[1]
    quarter = shard // 4
    pair = keyval_weight.shape[1]

    def half(weight, start, count):
        return lax.dynamic_slice(weight, (start, lane), (count, PAIR))

    depth, height = 8, sources // 8
    groups = [[y * depth + z for z in range(depth)] for y in range(height)]

    def along_z(piece):
        spread = jnp.broadcast_to(piece[None], (depth,) + piece.shape)
        return lax.all_to_all(spread, "seq", 0, 0, axis_index_groups=groups, tiled=True)

    piece = jnp.concatenate(
        [
            half(query_weight.T, chip * quarter, quarter),
            half(output_weight, chip * quarter, quarter),
        ],
        axis=0,
    )
    piece, patches, recompute_rows = after(piece, patches, recompute_rows)
    spread = along_z(piece)
    slab, cached, spread = after(half(keyval_weight.T, 0, pair), cached_keyval[0], spread)
    keyval_own = along_z(slab).reshape(depth * pair, PAIR)
    slim = depth * quarter
    small = jnp.concatenate(
        [
            spread[:, :quarter].reshape(slim, PAIR),
            spread[:, quarter:].reshape(slim, PAIR),
        ],
        axis=0,
    )
    column = lax.axis_index("seq") // depth
    small = around(small, shift_y)
    query_own = jnp.concatenate([v[:slim] for v in small], axis=0)
    output_own = jnp.concatenate([v[slim:] for v in small], axis=0)
    query_part = around(query_own, shift)
    query_other = [swap(w) for w in query_part]

    cached_before, cached_after = neighbours(cached)
    keyval_own, output_own, cached_before, cached_after = after(
        keyval_own, output_own, cached_before, cached_after
    )
    keyval_parts = around(keyval_own, shift_y)
    output_part = around(output_own, shift)
    m = lax.broadcasted_iota(jnp.int32, (width, width), 0)
    n = lax.broadcasted_iota(jnp.int32, (width, width), 1)

    def steps_of(place):
        return jnp.where(place == 2, 3, jnp.where(place == 3, 2, place))

    block = height * slim
    source_chip = (chip - steps_of(m // block) + 4) % 4
    source_column = (column - steps_of((m % block) // slim) + height) % height
    source = source_column * depth + (m % slim) // quarter
    natural = source * shard + source_chip * quarter + m % quarter
    reorder = (natural == n).astype(BF16)

    stream_in = patches[0].astype(F32)
    attention_in = layer_norm(stream_in).astype(BF16)
    picks = recompute_rows.shape[2]
    chosen = jnp.pad(recompute_rows[0, 0], (0, PICK - picks), constant_values=-1)
    row_of = lax.broadcasted_iota(jnp.int32, (PICK, rows), 1)
    chosen_rows = dot((chosen[:, None] == row_of).astype(BF16), attention_in).astype(BF16)
    segment_tag = jnp.repeat(group_segments[0], 4) + 1
    lines = rows // 128
    extra = jnp.concatenate(
        [
            jnp.pad(chosen[: PICK - lines, None].astype(BF16), ((0, 0), (0, 127))),
            segment_tag.astype(BF16).reshape(lines, 128),
        ],
        axis=0,
    )
    packet = jnp.concatenate([chosen_rows, extra], axis=1)
    packet_before, packet_after = neighbours(packet)

    def unpack(value):
        index = value[: PICK - lines, width].astype(jnp.int32)
        index = jnp.pad(index, (0, lines), constant_values=-1)
        return index, value[PICK - lines :, width:].reshape(rows).astype(jnp.int32)

    index_before, tag_before = unpack(packet_before)
    index_after, tag_after = unpack(packet_after)
    index = jnp.stack([index_before, chosen, index_after])
    key_tag = jnp.concatenate([tag_before, segment_tag, tag_after])


    keyval_full = jnp.zeros((sources * pair, PAIR), BF16)
    for steps, part in zip(ORDER, keyval_parts):
        place = ((column - steps + height) % height) * depth * pair
        keyval_full = lax.dynamic_update_slice(keyval_full, part, (place, 0))
    output_other = [swap(w) for w in output_part]

    other_lane = (width - PAIR) - lane
    in_own = lax.dynamic_slice(attention_in, (0, lane), (rows, PAIR))
    in_other = lax.dynamic_slice(attention_in, (0, other_lane), (rows, PAIR))
    at = lax.broadcasted_iota(jnp.int32, in_other.shape, 1) + other_lane
    shared = (at >= width - PAIR) & (at < PAIR)
    in_other = jnp.where(shared, jnp.zeros_like(in_other), in_other)
    queries = jnp.concatenate(
        [dot_t(in_own, a) + dot_t(in_other, b) for a, b in zip(query_part, query_other)], axis=1
    ).astype(BF16)
    queries = dot(queries, reorder).astype(BF16)

    picked = jnp.concatenate([packet_before, packet, packet_after], axis=0)[:, :width]
    both = jnp.concatenate([picked, swap(picked)], axis=0)
    both = lax.dynamic_slice(both, (0, lane), (both.shape[0], PAIR))
    keep = (lax.broadcasted_iota(jnp.int32, both.shape, 1) >= core * (2 * PAIR - width)).astype(BF16)
    both, queries = after(both * keep, queries)
    partial = dot_t(both, keyval_full)
    renewed = (partial[: 3 * PICK] + swap(partial[3 * PICK :])).astype(BF16)

    context = attend(
        queries, cached_before, cached, cached_after, renewed, index, segment_tag[:, None], key_tag[None]
    )
    context = dot_t(context, reorder).astype(BF16)
    out_own = dot(context, jnp.concatenate(output_part, axis=0))
    out_other = dot(context, jnp.concatenate(output_other, axis=0))
    left = jnp.where(core == 0, out_own, out_other)
    right = jnp.where(core == 0, out_other, out_own)
    attended = jnp.concatenate([left, right[:, 2 * PAIR - width :]], axis=1)
    stream = (stream_in + attended).astype(BF16)

    normed = layer_norm(stream.astype(F32)).astype(BF16)
    behind, ahead = shift(normed, 1), shift(normed, 3)
    weights = (expand_weight, reduce_weight)

    def other_part(value):
        return swap(feed(value, *weights))

    def chip_part(value, from_other):
        return feed(value, *weights, from_other)

    top, bottom = shift(behind[: rows // 2], 1), shift(ahead[rows // 2 :], 3)
    other_1, other_2 = swap(behind), swap(ahead)
    from_1 = other_part(other_1)
    from_2 = other_part(other_2)
    part_1 = chip_part(behind, from_1)
    back_1 = shift(part_1, 3)
    part_2 = chip_part(ahead, from_2)
    back_2 = shift(part_2, 1)
    top, bottom, normed, part_1, part_2 = after(top, bottom, normed, part_1, part_2)
    opposite = jnp.concatenate([top, bottom], axis=0)
    other_3 = swap(opposite)
    part_0 = chip_part(normed, other_part(swap(normed)))
    other_3, part_0 = after(other_3, part_0)
    from_3 = other_part(other_3)
    from_3, back_1, back_2 = after(from_3, back_1, back_2)
    back_3 = shift(chip_part(opposite, from_3), 2)
    total = part_0.astype(F32) + back_1.astype(F32) + back_2.astype(F32) + back_3.astype(F32)
    combined = stream.astype(F32) + total
    merged = layer_norm(combined).astype(BF16).reshape(rows // 4, 4 * width)

    destination = owners[0]
    count = destination.shape[0]
    capacity = 3 * count // sources
    same = destination[:, None] == destination[None, :]
    t = lax.broadcasted_iota(jnp.int32, (count, count), 0)
    u = lax.broadcasted_iota(jnp.int32, (count, count), 1)
    position = jnp.sum((same & (u < t)).astype(jnp.int32), axis=1)
    slot_index = (destination * capacity + position).reshape(8, count // 8)
    packs = jnp.stack(
        [2 * ((chip - j + 4) % 4) + c for j in ORDER for c in (core, 1 - core)]
    )
    slot_index = jnp.sum(
        jnp.where(packs[:, None, None] == jnp.arange(8)[None, :, None], slot_index[None], 0), axis=1
    ).reshape(count)
    dispatch = (
        slot_index[None, :] == lax.broadcasted_iota(jnp.int32, (sources * capacity, count), 0)
    ).astype(BF16)
    dispatch, merged = after(dispatch, merged)

    projected = []
    for value in around(merged, shift):
        pair = jnp.concatenate([value, swap(value)], axis=0)
        projected.append(dot(pair, merge_weight).astype(BF16))
    projected = jnp.concatenate(projected, axis=0)
    outgoing = dot(dispatch, projected).astype(BF16)
    outgoing = outgoing.reshape(sources, capacity, projected.shape[1])
    received = lax.all_to_all(outgoing, "seq", split_axis=0, concat_axis=0, tiled=True)
    return received[None]


def solution(mesh):
    return jax.shard_map(
        on_device,
        mesh=mesh,
        in_specs=(
            P("blk", "seq", None),
            P("blk", "seq"),
            P("blk", "seq", None),
            P("blk", "seq", None),
            P(None, "seq"),
            P(None, "seq"),
            P("seq", None),
            P(None, "blk"),
            P("blk", None),
            P(None, "blk"),
            P("seq", None),
        ),
        out_specs=P("seq", None, None, "blk"),
        check_vma=False,
    )
```

```python
import math

import jax
import jax.numpy as jnp
from jax import lax
from jax.experimental import pallas as pl
from jax.experimental.pallas import tpu as pltpu
from jax.sharding import PartitionSpec as P

HEADS = 16
HEAD = 88
PAIR = 768
PICK = 32
F32 = jnp.float32
BF16 = jnp.bfloat16
VM = pltpu.VMEM
ORDER = (0, 1, 3, 2)


def layer_norm(values):
    average = jnp.mean(values, axis=-1, keepdims=True)
    centered = values - average
    variance = jnp.mean(centered * centered, axis=-1, keepdims=True)
    return centered * lax.rsqrt(variance + 1e-06)


def swap(value):
    return lax.ppermute(value, "blk", [(b, b ^ 1) for b in range(8)])


def shift(value, steps):
    return lax.ppermute(value, "blk", [(b, (b + 2 * steps) % 8) for b in range(8)])


def neighbours(value):
    count = lax.axis_size("seq")
    up = [(i, i + 1) for i in range(count - 1)]
    before = lax.ppermute(value, "seq", up)
    after = lax.ppermute(value, "seq", [(j, i) for i, j in up])
    return before, after


def dot(a, b):
    return lax.dot_general(a, b, (((1,), (0,)), ((), ())), preferred_element_type=F32)


def dot_t(a, b):
    return lax.dot_general(a, b, (((1,), (1,)), ((), ())), preferred_element_type=F32)


def after(*values):
    return lax.optimization_barrier(values)


def shift_y(value, steps):
    count = lax.axis_size("seq")
    return lax.ppermute(value, "seq", [(s, (s + 8 * steps) % count) for s in range(count)])


def around(value, shift):
    behind, ahead = shift(value, 1), shift(value, 3)
    return [value, behind, ahead, across(behind, ahead, shift)]


def across(behind, ahead, shift):
    middle = behind.shape[0] // 2
    return jnp.concatenate([shift(behind[:middle], 1), shift(ahead[middle:], 3)], axis=0)


def feed_kernel(*refs):
    if len(refs) == 5:
        x_ref, e_ref, r_ref, add_ref, o_ref = refs
    else:
        x_ref, e_ref, r_ref, o_ref = refs
        add_ref = None
    units = e_ref.shape[1]
    x = x_ref[...]
    total = None
    for k in range(0, units, 256):
        inner = jnp.dot(x, e_ref[:, k:k+256], preferred_element_type=F32)
        hidden = (0.5 * inner * (1.0 + lax.erf(inner * math.sqrt(0.5)))).astype(BF16)
        part = jnp.dot(hidden, r_ref[k:k+256, :], preferred_element_type=F32)
        total = part if total is None else total + part
    if add_ref is not None:
        total = total + add_ref[...].astype(F32)
    o_ref[...] = total.astype(BF16)


def feed(x, e, r, add=None):
    args = (x, e, r) + (() if add is None else (add,))
    return pl.pallas_call(
        feed_kernel,
        out_shape=jax.ShapeDtypeStruct((x.shape[0], r.shape[1]), BF16),
        in_specs=[pl.BlockSpec(memory_space=VM)] * len(args),
        out_specs=pl.BlockSpec(memory_space=VM),
        compiler_params=pltpu.CompilerParams(vmem_limit_bytes=8 << 20),
        cost_estimate=pl.CostEstimate(
            flops=x.size,
            transcendentals=0,
            bytes_accessed=2 * (2 * x.size + e.size + r.size),
        ),
    )(*args)


def attend_kernel(q_ref, before_ref, own_ref, after_ref, fresh_ref, index_ref, qtag_ref, ktag_ref, o_ref, kv_ref, acc_ref):
    rows, width = q_ref.shape
    for b, old in enumerate((before_ref, own_ref, after_ref)):
        at = lax.broadcasted_iota(jnp.int32, (rows, PICK), 0)
        hit = (index_ref[b:b+1, :] == at).astype(F32)
        any_hit = jnp.max(hit, axis=1, keepdims=True) > 0.0
        hit = hit.astype(BF16)
        for k in range(0, 2*width, 256):
            new = jnp.dot(hit, fresh_ref[b*PICK:(b+1)*PICK, k:k+256], preferred_element_type=F32)
            kv_ref[b*rows:(b+1)*rows, k:k+256] = jnp.where(any_hit, new, old[:, k:k+256].astype(F32)).astype(BF16)
    allowed = qtag_ref[...] == ktag_ref[...]
    scale = 1.0 / math.sqrt(HEAD)
    for h in range(HEADS):
        lo = (HEAD*h)//128*128
        hi = -(-(HEAD*(h+1))//128)*128
        lane = lax.broadcasted_iota(jnp.int32, (rows, hi-lo), 1) + lo
        mine = (lane >= HEAD*h) & (lane < HEAD*(h+1))
        q = q_ref[:, lo:hi]
        q = jnp.where(mine, q.astype(F32), 0.0).astype(BF16)
        s = lax.dot_general(q, kv_ref[:, lo:hi], (((1,),(1,)),((),())), preferred_element_type=F32)
        s = jnp.where(allowed, s, -1e30)
        top = jnp.max(s, axis=1, keepdims=True)
        raised = jnp.exp((s - top) * scale)
        total = jnp.sum(raised, axis=1, keepdims=True)
        o = jnp.dot(raised.astype(BF16), kv_ref[:, width+lo:width+hi], preferred_element_type=F32)
        o = o / total
        acc_ref[:, lo:hi] = jnp.where(mine, o, acc_ref[:, lo:hi])
    o_ref[...] = acc_ref[...].astype(BF16)


def attend(q, before, own, after, fresh, index, qtag, ktag):
    rows, width = q.shape
    return pl.pallas_call(
        attend_kernel,
        out_shape=jax.ShapeDtypeStruct((rows, width), BF16),
        in_specs=[pl.BlockSpec(memory_space=VM)] * 8,
        out_specs=pl.BlockSpec(memory_space=VM),
        scratch_shapes=[VM((3*rows, 2*width), BF16), VM((rows, width), F32)],
        compiler_params=pltpu.CompilerParams(vmem_limit_bytes=24 << 20),
        cost_estimate=pl.CostEstimate(
            flops=12 * rows * rows * width,
            transcendentals=3 * HEADS * rows * rows,
            bytes_accessed=2 * (2 * q.size + 3 * own.size),
        ),
    )(q, before, own, after, fresh, index, qtag, ktag)


def on_device(
    patches,
    group_segments,
    cached_keyval,
    recompute_rows,
    query_weight,
    keyval_weight,
    output_weight,
    expand_weight,
    reduce_weight,
    merge_weight,
    owners,
):
    rows = patches.shape[1]
    width = patches.shape[2]
    blk = lax.axis_index("blk")
    chip, core = blk // 2, blk % 2
    sources = lax.axis_size("seq")

    lane = core * (width - PAIR)
    shard = query_weight.shape[1]
    quarter = shard // 4
    pair = keyval_weight.shape[1]

    def half(weight, start, count):
        return lax.dynamic_slice(weight, (start, lane), (count, PAIR))

    depth, height = 8, sources // 8
    groups = [[y * depth + z for z in range(depth)] for y in range(height)]

    def copies(piece):
        return jnp.broadcast_to(piece[None], (depth,) + piece.shape)

    def along_z(spread):
        return lax.all_to_all(spread, "seq", 0, 0, axis_index_groups=groups, tiled=True)

    piece = jnp.concatenate(
        [
            half(query_weight.T, chip * quarter, quarter),
            half(output_weight, chip * quarter, quarter),
        ],
        axis=0,
    )
    piece, slab = copies(piece), copies(half(keyval_weight.T, 0, pair))
    piece, slab, patches, recompute_rows = after(piece, slab, patches, recompute_rows)
    spread = along_z(piece)
    keyval_own = along_z(slab).reshape(depth * pair, PAIR)
    cached = cached_keyval[0]
    cached_before, cached_after = neighbours(cached)
    slim = depth * quarter
    small = jnp.concatenate(
        [
            spread[:, :quarter].reshape(slim, PAIR),
            spread[:, quarter:].reshape(slim, PAIR),
        ],
        axis=0,
    )
    column = lax.axis_index("seq") // depth
    small = around(small, shift_y)
    query_own = jnp.concatenate([v[:slim] for v in small], axis=0)
    output_own = jnp.concatenate([v[slim:] for v in small], axis=0)
    query_own, output_own, keyval_own, cached_before, cached_after = after(
        query_own, output_own, keyval_own, cached_before, cached_after
    )
    keyval_parts = around(keyval_own, shift_y)
    query_part = around(query_own, shift)
    output_part = around(output_own, shift)
    query_other = [swap(w) for w in query_part]
    output_other = [swap(w) for w in output_part]
    column, query_own = after(column, query_own)
    m = lax.broadcasted_iota(jnp.int32, (width, width), 0)
    n = lax.broadcasted_iota(jnp.int32, (width, width), 1)

    def steps_of(place):
        return jnp.where(place == 2, 3, jnp.where(place == 3, 2, place))

    block = height * slim
    source_chip = (chip - steps_of(m // block) + 4) % 4
    source_column = (column - steps_of((m % block) // slim) + height) % height
    source = source_column * depth + (m % slim) // quarter
    natural = source * shard + source_chip * quarter + m % quarter
    reorder = (natural == n).astype(BF16)

    stream_in = patches[0].astype(F32)
    attention_in = layer_norm(stream_in).astype(BF16)
    picks = recompute_rows.shape[2]
    chosen = jnp.pad(recompute_rows[0, 0], (0, PICK - picks), constant_values=-1)
    row_of = lax.broadcasted_iota(jnp.int32, (PICK, rows), 1)
    chosen_rows = dot((chosen[:, None] == row_of).astype(BF16), attention_in).astype(BF16)
    segment_tag = jnp.repeat(group_segments[0], 4) + 1
    lines = rows // 128
    extra = jnp.concatenate(
        [
            jnp.pad(chosen[: PICK - lines, None].astype(BF16), ((0, 0), (0, 127))),
            segment_tag.astype(BF16).reshape(lines, 128),
        ],
        axis=0,
    )
    packet = jnp.concatenate([chosen_rows, extra], axis=1)
    packet_before, packet_after = neighbours(packet)

    def unpack(value):
        index = value[: PICK - lines, width].astype(jnp.int32)
        index = jnp.pad(index, (0, lines), constant_values=-1)
        return index, value[PICK - lines :, width:].reshape(rows).astype(jnp.int32)

    index_before, tag_before = unpack(packet_before)
    index_after, tag_after = unpack(packet_after)
    index = jnp.stack([index_before, chosen, index_after])
    key_tag = jnp.concatenate([tag_before, segment_tag, tag_after])


    keyval_full = jnp.zeros((sources * pair, PAIR), BF16)
    for steps, part in zip(ORDER, keyval_parts):
        place = ((column - steps + height) % height) * depth * pair
        keyval_full = lax.dynamic_update_slice(keyval_full, part, (place, 0))

    other_lane = (width - PAIR) - lane
    in_own = lax.dynamic_slice(attention_in, (0, lane), (rows, PAIR))
    in_other = lax.dynamic_slice(attention_in, (0, other_lane), (rows, PAIR))
    at = lax.broadcasted_iota(jnp.int32, in_other.shape, 1) + other_lane
    shared = (at >= width - PAIR) & (at < PAIR)
    in_other = jnp.where(shared, jnp.zeros_like(in_other), in_other)
    queries = jnp.concatenate(
        [dot_t(in_own, a) + dot_t(in_other, b) for a, b in zip(query_part, query_other)], axis=1
    ).astype(BF16)
    queries = dot(queries, reorder).astype(BF16)

    picked = jnp.concatenate([packet_before, packet, packet_after], axis=0)[:, :width]
    both = jnp.concatenate([picked, swap(picked)], axis=0)
    both = lax.dynamic_slice(both, (0, lane), (both.shape[0], PAIR))
    keep = (lax.broadcasted_iota(jnp.int32, both.shape, 1) >= core * (2 * PAIR - width)).astype(BF16)
    both, queries = after(both * keep, queries)
    partial = dot_t(both, keyval_full)
    renewed = (partial[: 3 * PICK] + swap(partial[3 * PICK :])).astype(BF16)

    context = attend(
        queries, cached_before, cached, cached_after, renewed, index, segment_tag[:, None], key_tag[None]
    )
    context = dot_t(context, reorder).astype(BF16)
    out_own = dot(context, jnp.concatenate(output_part, axis=0))
    out_other = dot(context, jnp.concatenate(output_other, axis=0))
    left = jnp.where(core == 0, out_own, out_other)
    right = jnp.where(core == 0, out_other, out_own)
    attended = jnp.concatenate([left, right[:, 2 * PAIR - width :]], axis=1)
    stream = (stream_in + attended).astype(BF16)

    normed = layer_norm(stream.astype(F32)).astype(BF16)
    behind, ahead = shift(normed, 1), shift(normed, 3)
    weights = (expand_weight, reduce_weight)

    def other_part(value):
        return swap(feed(value, *weights))

    def chip_part(value, from_other):
        return feed(value, *weights, from_other)

    top, bottom = shift(behind[: rows // 2], 1), shift(ahead[rows // 2 :], 3)
    other_1, other_2 = swap(behind), swap(ahead)
    from_1 = other_part(other_1)
    from_2 = other_part(other_2)
    top, bottom, from_1, from_2 = after(top, bottom, from_1, from_2)
    part_1 = chip_part(behind, from_1)
    back_1 = shift(part_1, 3)
    part_2 = chip_part(ahead, from_2)
    back_2 = shift(part_2, 1)
    other_3 = swap(jnp.concatenate([top, bottom], axis=0))
    opposite = jnp.concatenate([top, bottom], axis=0)
    normed, other_3, part_1, part_2 = after(normed, other_3, part_1, part_2)
    other_0 = swap(normed)
    from_3 = other_part(other_3)
    other_0, from_3 = after(other_0, from_3)
    from_0 = other_part(other_0)
    part_3 = chip_part(opposite, from_3)
    back_3 = shift(part_3, 2)
    from_0, part_3 = after(from_0, part_3)
    part_0 = chip_part(normed, from_0)
    total = part_0.astype(F32) + back_1.astype(F32) + back_2.astype(F32) + back_3.astype(F32)
    combined = stream.astype(F32) + total
    merged = layer_norm(combined).astype(BF16).reshape(rows // 4, 4 * width)

    destination = owners[0]
    count = destination.shape[0]
    capacity = 3 * count // sources
    same = destination[:, None] == destination[None, :]
    t = lax.broadcasted_iota(jnp.int32, (count, count), 0)
    u = lax.broadcasted_iota(jnp.int32, (count, count), 1)
    position = jnp.sum((same & (u < t)).astype(jnp.int32), axis=1)
    slot_index = (destination * capacity + position).reshape(8, count // 8)
    packs = jnp.stack(
        [2 * ((chip - j + 4) % 4) + c for j in ORDER for c in (core, 1 - core)]
    )
    slot_index = jnp.sum(
        jnp.where(packs[:, None, None] == jnp.arange(8)[None, :, None], slot_index[None], 0), axis=1
    ).reshape(count)
    dispatch = (
        slot_index[None, :] == lax.broadcasted_iota(jnp.int32, (sources * capacity, count), 0)
    ).astype(BF16)
    dispatch, merged = after(dispatch, merged)

    projected = []
    for value in around(merged, shift):
        pair = jnp.concatenate([value, swap(value)], axis=0)
        projected.append(dot(pair, merge_weight).astype(BF16))
    projected = jnp.concatenate(projected, axis=0)
    outgoing = dot(dispatch, projected).astype(BF16)
    outgoing = outgoing.reshape(sources, capacity, projected.shape[1])
    received = lax.all_to_all(outgoing, "seq", split_axis=0, concat_axis=0, tiled=True)
    return received[None]


def solution(mesh):
    return jax.shard_map(
        on_device,
        mesh=mesh,
        in_specs=(
            P("blk", "seq", None),
            P("blk", "seq"),
            P("blk", "seq", None),
            P("blk", "seq", None),
            P(None, "seq"),
            P(None, "seq"),
            P("seq", None),
            P(None, "blk"),
            P("blk", None),
            P(None, "blk"),
            P("seq", None),
        ),
        out_specs=P("seq", None, None, "blk"),
        check_vma=False,
    )
```

```python
import math

import jax
import jax.numpy as jnp
from jax import lax
from jax.experimental import pallas as pl
from jax.experimental.pallas import tpu as pltpu
from jax.sharding import PartitionSpec as P

HEADS = 16
HEAD = 88
PAIR = 768
PICK = 32
F32 = jnp.float32
BF16 = jnp.bfloat16
VM = pltpu.VMEM
ORDER = (0, 1, 3, 2)


def layer_norm(values):
    average = jnp.mean(values, axis=-1, keepdims=True)
    centered = values - average
    variance = jnp.mean(centered * centered, axis=-1, keepdims=True)
    return centered * lax.rsqrt(variance + 1e-06)


def swap(value):
    return lax.ppermute(value, "blk", [(b, b ^ 1) for b in range(8)])


def shift(value, steps):
    return lax.ppermute(value, "blk", [(b, (b + 2 * steps) % 8) for b in range(8)])


def neighbours(value):
    count = lax.axis_size("seq")
    up = [(i, i + 1) for i in range(count - 1)]
    before = lax.ppermute(value, "seq", up)
    after = lax.ppermute(value, "seq", [(j, i) for i, j in up])
    return before, after


def dot(a, b):
    return lax.dot_general(a, b, (((1,), (0,)), ((), ())), preferred_element_type=F32)


def dot_t(a, b):
    return lax.dot_general(a, b, (((1,), (1,)), ((), ())), preferred_element_type=F32)


def after(*values):
    return lax.optimization_barrier(values)


def shift_y(value, steps):
    count = lax.axis_size("seq")
    return lax.ppermute(value, "seq", [(s, (s + 8 * steps) % count) for s in range(count)])


def around(value, shift):
    behind, ahead = shift(value, 1), shift(value, 3)
    return [value, behind, ahead, across(behind, ahead, shift)]


def across(behind, ahead, shift):
    middle = behind.shape[0] // 2
    return jnp.concatenate([shift(behind[:middle], 1), shift(ahead[middle:], 3)], axis=0)


def feed_kernel(*refs):
    if len(refs) == 5:
        x_ref, e_ref, r_ref, add_ref, o_ref = refs
    else:
        x_ref, e_ref, r_ref, o_ref = refs
        add_ref = None
    units = e_ref.shape[1]
    x = x_ref[...]
    total = None
    for k in range(0, units, 256):
        inner = jnp.dot(x, e_ref[:, k:k+256], preferred_element_type=F32)
        hidden = (0.5 * inner * (1.0 + lax.erf(inner * math.sqrt(0.5)))).astype(BF16)
        part = jnp.dot(hidden, r_ref[k:k+256, :], preferred_element_type=F32)
        total = part if total is None else total + part
    if add_ref is not None:
        total = total + add_ref[...].astype(F32)
    o_ref[...] = total.astype(BF16)


def feed(x, e, r, add=None):
    args = (x, e, r) + (() if add is None else (add,))
    return pl.pallas_call(
        feed_kernel,
        out_shape=jax.ShapeDtypeStruct((x.shape[0], r.shape[1]), BF16),
        in_specs=[pl.BlockSpec(memory_space=VM)] * len(args),
        out_specs=pl.BlockSpec(memory_space=VM),
        compiler_params=pltpu.CompilerParams(vmem_limit_bytes=8 << 20),
        cost_estimate=pl.CostEstimate(
            flops=x.size,
            transcendentals=0,
            bytes_accessed=x.size,
        ),
    )(*args)


def attend_kernel(q_ref, before_ref, own_ref, after_ref, fresh_ref, index_ref, qtag_ref, ktag_ref, o_ref, kv_ref, acc_ref):
    rows, width = q_ref.shape
    for b, old in enumerate((before_ref, own_ref, after_ref)):
        at = lax.broadcasted_iota(jnp.int32, (rows, PICK), 0)
        hit = (index_ref[b:b+1, :] == at).astype(F32)
        any_hit = jnp.max(hit, axis=1, keepdims=True) > 0.0
        hit = hit.astype(BF16)
        for k in range(0, 2*width, 256):
            new = jnp.dot(hit, fresh_ref[b*PICK:(b+1)*PICK, k:k+256], preferred_element_type=F32)
            kv_ref[b*rows:(b+1)*rows, k:k+256] = jnp.where(any_hit, new, old[:, k:k+256].astype(F32)).astype(BF16)
    allowed = qtag_ref[...] == ktag_ref[...]
    scale = 1.0 / math.sqrt(HEAD)
    for h in range(HEADS):
        lo = (HEAD*h)//128*128
        hi = -(-(HEAD*(h+1))//128)*128
        lane = lax.broadcasted_iota(jnp.int32, (rows, hi-lo), 1) + lo
        mine = (lane >= HEAD*h) & (lane < HEAD*(h+1))
        q = q_ref[:, lo:hi]
        q = jnp.where(mine, q.astype(F32), 0.0).astype(BF16)
        s = lax.dot_general(q, kv_ref[:, lo:hi], (((1,),(1,)),((),())), preferred_element_type=F32)
        s = jnp.where(allowed, s, -1e30)
        top = jnp.max(s, axis=1, keepdims=True)
        raised = jnp.exp((s - top) * scale)
        total = jnp.sum(raised, axis=1, keepdims=True)
        o = jnp.dot(raised.astype(BF16), kv_ref[:, width+lo:width+hi], preferred_element_type=F32)
        o = o / total
        acc_ref[:, lo:hi] = jnp.where(mine, o, acc_ref[:, lo:hi])
    o_ref[...] = acc_ref[...].astype(BF16)


def attend(q, before, own, after, fresh, index, qtag, ktag):
    rows, width = q.shape
    return pl.pallas_call(
        attend_kernel,
        out_shape=jax.ShapeDtypeStruct((rows, width), BF16),
        in_specs=[pl.BlockSpec(memory_space=VM)] * 8,
        out_specs=pl.BlockSpec(memory_space=VM),
        scratch_shapes=[VM((3*rows, 2*width), BF16), VM((rows, width), F32)],
        compiler_params=pltpu.CompilerParams(vmem_limit_bytes=24 << 20),
        cost_estimate=pl.CostEstimate(
            flops=q.size,
            transcendentals=0,
            bytes_accessed=q.size,
        ),
    )(q, before, own, after, fresh, index, qtag, ktag)


def on_device(
    patches,
    group_segments,
    cached_keyval,
    recompute_rows,
    query_weight,
    keyval_weight,
    output_weight,
    expand_weight,
    reduce_weight,
    merge_weight,
    owners,
):
    rows = patches.shape[1]
    width = patches.shape[2]
    blk = lax.axis_index("blk")
    chip, core = blk // 2, blk % 2
    sources = lax.axis_size("seq")

    lane = core * (width - PAIR)
    shard = query_weight.shape[1]
    quarter = shard // 4
    pair = keyval_weight.shape[1]

    def half(weight, start, count):
        return lax.dynamic_slice(weight, (start, lane), (count, PAIR))

    depth, height = 8, sources // 8
    groups = [[y * depth + z for z in range(depth)] for y in range(height)]

    def copies(piece):
        return jnp.broadcast_to(piece[None], (depth,) + piece.shape)

    def along_z(spread):
        return lax.all_to_all(spread, "seq", 0, 0, axis_index_groups=groups, tiled=True)

    piece = jnp.concatenate(
        [
            half(query_weight.T, chip * quarter, quarter),
            half(output_weight, chip * quarter, quarter),
        ],
        axis=0,
    )
    piece, slab = copies(piece), copies(half(keyval_weight.T, 0, pair))
    piece, slab, patches, recompute_rows, merge_start = after(
        piece, slab, patches, recompute_rows, merge_weight
    )
    spread = along_z(piece)
    keyval_own = along_z(slab).reshape(depth * pair, PAIR)
    cached = cached_keyval[0]
    cached_before, cached_after = neighbours(cached)
    merge_behind, merge_ahead = shift(merge_start, 1), shift(merge_start, 3)
    slim = depth * quarter
    small = jnp.concatenate(
        [
            spread[:, :quarter].reshape(slim, PAIR),
            spread[:, quarter:].reshape(slim, PAIR),
        ],
        axis=0,
    )
    column = lax.axis_index("seq") // depth
    small = around(small, shift_y)
    query_own = jnp.concatenate([v[:slim] for v in small], axis=0)
    output_own = jnp.concatenate([v[slim:] for v in small], axis=0)
    (
        query_own,
        output_own,
        keyval_own,
        cached_before,
        cached_after,
        merge_behind,
        merge_ahead,
    ) = after(
        query_own, output_own, keyval_own, cached_before, cached_after, merge_behind, merge_ahead
    )
    keyval_parts = around(keyval_own, shift_y)
    behind, ahead = shift(query_own, 1), shift(query_own, 3)
    keyval_parts[1], keyval_parts[2], behind, ahead = after(
        keyval_parts[1], keyval_parts[2], behind, ahead
    )
    query_part = [query_own, behind, ahead, across(behind, ahead, shift)]
    output_part = around(output_own, shift)
    query_other = [swap(w) for w in query_part]
    output_other = [swap(w) for w in output_part]
    column, query_own = after(column, query_own)
    m = lax.broadcasted_iota(jnp.int32, (width, width), 0)
    n = lax.broadcasted_iota(jnp.int32, (width, width), 1)

    def steps_of(place):
        return jnp.where(place == 2, 3, jnp.where(place == 3, 2, place))

    block = height * slim
    source_chip = (chip - steps_of(m // block) + 4) % 4
    source_column = (column - steps_of((m % block) // slim) + height) % height
    source = source_column * depth + (m % slim) // quarter
    natural = source * shard + source_chip * quarter + m % quarter
    reorder = (natural == n).astype(BF16)

    stream_in = patches[0].astype(F32)
    attention_in = layer_norm(stream_in).astype(BF16)
    picks = recompute_rows.shape[2]
    chosen = jnp.pad(recompute_rows[0, 0], (0, PICK - picks), constant_values=-1)
    row_of = lax.broadcasted_iota(jnp.int32, (PICK, rows), 1)
    chosen_rows = dot((chosen[:, None] == row_of).astype(BF16), attention_in).astype(BF16)
    segment_tag = jnp.repeat(group_segments[0], 4) + 1
    lines = rows // 128
    extra = jnp.concatenate(
        [
            jnp.pad(chosen[: PICK - lines, None].astype(BF16), ((0, 0), (0, 127))),
            segment_tag.astype(BF16).reshape(lines, 128),
        ],
        axis=0,
    )
    packet = jnp.concatenate([chosen_rows, extra], axis=1)
    packet_before, packet_after = neighbours(packet)

    def unpack(value):
        index = value[: PICK - lines, width].astype(jnp.int32)
        index = jnp.pad(index, (0, lines), constant_values=-1)
        return index, value[PICK - lines :, width:].reshape(rows).astype(jnp.int32)

    index_before, tag_before = unpack(packet_before)
    index_after, tag_after = unpack(packet_after)
    index = jnp.stack([index_before, chosen, index_after])
    key_tag = jnp.concatenate([tag_before, segment_tag, tag_after])


    keyval_full = jnp.zeros((sources * pair, PAIR), BF16)
    for steps, part in zip(ORDER, keyval_parts):
        place = ((column - steps + height) % height) * depth * pair
        keyval_full = lax.dynamic_update_slice(keyval_full, part, (place, 0))

    other_lane = (width - PAIR) - lane
    in_own = lax.dynamic_slice(attention_in, (0, lane), (rows, PAIR))
    in_other = lax.dynamic_slice(attention_in, (0, other_lane), (rows, PAIR))
    at = lax.broadcasted_iota(jnp.int32, in_other.shape, 1) + other_lane
    shared = (at >= width - PAIR) & (at < PAIR)
    in_other = jnp.where(shared, jnp.zeros_like(in_other), in_other)
    queries = jnp.concatenate(
        [dot_t(in_own, a) + dot_t(in_other, b) for a, b in zip(query_part, query_other)], axis=1
    ).astype(BF16)
    queries = dot(queries, reorder).astype(BF16)

    picked = jnp.concatenate([packet_before, packet, packet_after], axis=0)[:, :width]
    both = jnp.concatenate([picked, swap(picked)], axis=0)
    both = lax.dynamic_slice(both, (0, lane), (both.shape[0], PAIR))
    keep = (lax.broadcasted_iota(jnp.int32, both.shape, 1) >= core * (2 * PAIR - width)).astype(BF16)
    both, queries, merge_behind, merge_ahead, *output_other = after(
        both * keep, queries, merge_behind, merge_ahead, *output_other
    )
    middle = merge_weight.shape[0] // 2
    merge_top = shift(merge_behind[:middle], 1)
    merge_bottom = shift(merge_ahead[middle:], 3)
    partial = dot_t(both, keyval_full)
    renewed = (partial[: 3 * PICK] + swap(partial[3 * PICK :])).astype(BF16)

    context = attend(
        queries, cached_before, cached, cached_after, renewed, index, segment_tag[:, None], key_tag[None]
    )
    context = dot_t(context, reorder).astype(BF16)
    out_own = dot(context, jnp.concatenate(output_part, axis=0))
    out_other = dot(context, jnp.concatenate(output_other, axis=0))
    left = jnp.where(core == 0, out_own, out_other)
    right = jnp.where(core == 0, out_other, out_own)
    attended = jnp.concatenate([left, right[:, 2 * PAIR - width :]], axis=1)
    stream = (stream_in + attended).astype(BF16)

    normed = layer_norm(stream.astype(F32)).astype(BF16)
    normed, merge_top, merge_bottom = after(normed, merge_top, merge_bottom)
    behind, ahead = shift(normed, 1), shift(normed, 3)
    weights = (expand_weight, reduce_weight)

    def other_part(value):
        return swap(feed(value, *weights))

    def chip_part(value, from_other):
        return feed(value, *weights, from_other)

    top, bottom = shift(behind[: rows // 2], 1), shift(ahead[rows // 2 :], 3)
    other_1, other_2 = swap(behind), swap(ahead)
    from_1 = other_part(other_1)
    from_2 = other_part(other_2)
    top, bottom, from_1, from_2 = after(top, bottom, from_1, from_2)
    part_1 = chip_part(behind, from_1)
    back_1 = shift(part_1, 3)
    part_2 = chip_part(ahead, from_2)
    back_2 = shift(part_2, 1)
    other_3 = swap(jnp.concatenate([top, bottom], axis=0))
    opposite = jnp.concatenate([top, bottom], axis=0)
    other_3, part_1, part_2 = after(other_3, part_1, part_2)
    other_0 = swap(normed)
    from_3 = other_part(other_3)
    other_0, from_3 = after(other_0, from_3)
    from_0 = other_part(other_0)
    part_3 = chip_part(opposite, from_3)
    back_3 = shift(part_3, 2)
    from_0, part_3 = after(from_0, part_3)
    part_0 = chip_part(normed, from_0)
    total = part_0.astype(F32) + back_1.astype(F32) + back_2.astype(F32) + back_3.astype(F32)
    combined = stream.astype(F32) + total
    merged = layer_norm(combined).astype(BF16).reshape(rows // 4, 4 * width)

    destination = owners[0]
    count = destination.shape[0]
    capacity = 3 * count // sources
    same = destination[:, None] == destination[None, :]
    t = lax.broadcasted_iota(jnp.int32, (count, count), 0)
    u = lax.broadcasted_iota(jnp.int32, (count, count), 1)
    position = jnp.sum((same & (u < t)).astype(jnp.int32), axis=1)
    slot_index = (destination * capacity + position).reshape(8, count // 8)
    packs = jnp.stack(
        [2 * ((chip - j + 4) % 4) + c for j in ORDER for c in (core, 1 - core)]
    )
    slot_index = jnp.sum(
        jnp.where(packs[:, None, None] == jnp.arange(8)[None, :, None], slot_index[None], 0), axis=1
    ).reshape(count)
    dispatch = (
        slot_index[None, :] == lax.broadcasted_iota(jnp.int32, (sources * capacity, count), 0)
    ).astype(BF16)
    dispatch, merged = after(dispatch, merged)

    both_packs = jnp.concatenate([merged, swap(merged)], axis=0)
    far = dot(both_packs[:, :middle], merge_top) + dot(both_packs[:, middle:], merge_bottom)
    projected = jnp.concatenate(
        [
            dot(both_packs, merge_weight).astype(BF16),
            shift(dot(both_packs, merge_ahead).astype(BF16), 1),
            shift(dot(both_packs, merge_behind).astype(BF16), 3),
            shift(far.astype(BF16), 2),
        ],
        axis=0,
    )
    outgoing = dot(dispatch, projected).astype(BF16)
    outgoing = outgoing.reshape(sources, capacity, projected.shape[1])
    received = lax.all_to_all(outgoing, "seq", split_axis=0, concat_axis=0, tiled=True)
    return received[None]


def solution(mesh):
    return jax.shard_map(
        on_device,
        mesh=mesh,
        in_specs=(
            P("blk", "seq", None),
            P("blk", "seq"),
            P("blk", "seq", None),
            P("blk", "seq", None),
            P(None, "seq"),
            P(None, "seq"),
            P("seq", None),
            P(None, "blk"),
            P("blk", None),
            P(None, "blk"),
            P("seq", None),
        ),
        out_specs=P("seq", None, None, "blk"),
        check_vma=False,
    )
```

```python
import math

import jax
import jax.numpy as jnp
from jax import lax
from jax.experimental import pallas as pl
from jax.experimental.pallas import tpu as pltpu
from jax.sharding import PartitionSpec as P

HEADS = 16
HEAD = 88
PAIR = 768
PICK = 32
F32 = jnp.float32
BF16 = jnp.bfloat16
VM = pltpu.VMEM
ORDER = (0, 1, 3, 2)


def layer_norm(values):
    average = jnp.mean(values, axis=-1, keepdims=True)
    centered = values - average
    variance = jnp.mean(centered * centered, axis=-1, keepdims=True)
    return centered * lax.rsqrt(variance + 1e-06)


def swap(value):
    return lax.ppermute(value, "blk", [(b, b ^ 1) for b in range(8)])


def shift(value, steps):
    return lax.ppermute(value, "blk", [(b, (b + 2 * steps) % 8) for b in range(8)])


def neighbours(value):
    count = lax.axis_size("seq")
    up = [(i, i + 1) for i in range(count - 1)]
    before = lax.ppermute(value, "seq", up)
    after = lax.ppermute(value, "seq", [(j, i) for i, j in up])
    return before, after


def dot(a, b):
    return lax.dot_general(a, b, (((1,), (0,)), ((), ())), preferred_element_type=F32)


def dot_t(a, b):
    return lax.dot_general(a, b, (((1,), (1,)), ((), ())), preferred_element_type=F32)


def after(*values):
    return lax.optimization_barrier(values)


def shift_y(value, steps):
    count = lax.axis_size("seq")
    return lax.ppermute(value, "seq", [(s, (s + 8 * steps) % count) for s in range(count)])


def around(value, shift):
    behind, ahead = shift(value, 1), shift(value, 3)
    return [value, behind, ahead, across(behind, ahead, shift)]


def across(behind, ahead, shift):
    middle = behind.shape[0] // 2
    return jnp.concatenate([shift(behind[:middle], 1), shift(ahead[middle:], 3)], axis=0)


def feed_kernel(*refs):
    if len(refs) == 5:
        x_ref, e_ref, r_ref, add_ref, o_ref = refs
    else:
        x_ref, e_ref, r_ref, o_ref = refs
        add_ref = None
    units = e_ref.shape[1]
    x = x_ref[...]
    total = None
    for k in range(0, units, 256):
        inner = jnp.dot(x, e_ref[:, k:k+256], preferred_element_type=F32)
        hidden = (0.5 * inner * (1.0 + lax.erf(inner * math.sqrt(0.5)))).astype(BF16)
        part = jnp.dot(hidden, r_ref[k:k+256, :], preferred_element_type=F32)
        total = part if total is None else total + part
    if add_ref is not None:
        total = total + add_ref[...].astype(F32)
    o_ref[...] = total.astype(BF16)


def feed(x, e, r, add=None):
    args = (x, e, r) + (() if add is None else (add,))
    return pl.pallas_call(
        feed_kernel,
        out_shape=jax.ShapeDtypeStruct((x.shape[0], r.shape[1]), BF16),
        in_specs=[pl.BlockSpec(memory_space=VM)] * len(args),
        out_specs=pl.BlockSpec(memory_space=VM),
        compiler_params=pltpu.CompilerParams(vmem_limit_bytes=8 << 20),
        cost_estimate=pl.CostEstimate(
            flops=x.size,
            transcendentals=0,
            bytes_accessed=2 * (2 * x.size + e.size + r.size),
        ),
    )(*args)


def attend_kernel(q_ref, before_ref, own_ref, after_ref, fresh_ref, index_ref, qtag_ref, ktag_ref, o_ref, kv_ref, acc_ref):
    rows, width = q_ref.shape
    for b, old in enumerate((before_ref, own_ref, after_ref)):
        at = lax.broadcasted_iota(jnp.int32, (rows, PICK), 0)
        hit = (index_ref[b:b+1, :] == at).astype(F32)
        any_hit = jnp.max(hit, axis=1, keepdims=True) > 0.0
        hit = hit.astype(BF16)
        for k in range(0, 2*width, 256):
            new = jnp.dot(hit, fresh_ref[b*PICK:(b+1)*PICK, k:k+256], preferred_element_type=F32)
            kv_ref[b*rows:(b+1)*rows, k:k+256] = jnp.where(any_hit, new, old[:, k:k+256].astype(F32)).astype(BF16)
    allowed = qtag_ref[...] == ktag_ref[...]
    scale = 1.0 / math.sqrt(HEAD)
    for h in range(HEADS):
        lo = (HEAD*h)//128*128
        hi = -(-(HEAD*(h+1))//128)*128
        lane = lax.broadcasted_iota(jnp.int32, (rows, hi-lo), 1) + lo
        mine = (lane >= HEAD*h) & (lane < HEAD*(h+1))
        q = q_ref[:, lo:hi]
        q = jnp.where(mine, q.astype(F32), 0.0).astype(BF16)
        s = lax.dot_general(q, kv_ref[:, lo:hi], (((1,),(1,)),((),())), preferred_element_type=F32)
        s = jnp.where(allowed, s, -1e30)
        top = jnp.max(s, axis=1, keepdims=True)
        raised = jnp.exp((s - top) * scale)
        total = jnp.sum(raised, axis=1, keepdims=True)
        o = jnp.dot(raised.astype(BF16), kv_ref[:, width+lo:width+hi], preferred_element_type=F32)
        o = o / total
        acc_ref[:, lo:hi] = jnp.where(mine, o, acc_ref[:, lo:hi])
    o_ref[...] = acc_ref[...].astype(BF16)


def attend(q, before, own, after, fresh, index, qtag, ktag):
    rows, width = q.shape
    return pl.pallas_call(
        attend_kernel,
        out_shape=jax.ShapeDtypeStruct((rows, width), BF16),
        in_specs=[pl.BlockSpec(memory_space=VM)] * 8,
        out_specs=pl.BlockSpec(memory_space=VM),
        scratch_shapes=[VM((3*rows, 2*width), BF16), VM((rows, width), F32)],
        compiler_params=pltpu.CompilerParams(vmem_limit_bytes=24 << 20),
        cost_estimate=pl.CostEstimate(
            flops=12 * rows * rows * width,
            transcendentals=3 * HEADS * rows * rows,
            bytes_accessed=2 * (2 * q.size + 3 * own.size),
        ),
    )(q, before, own, after, fresh, index, qtag, ktag)


def on_device(
    patches,
    group_segments,
    cached_keyval,
    recompute_rows,
    query_weight,
    keyval_weight,
    output_weight,
    expand_weight,
    reduce_weight,
    merge_weight,
    owners,
):
    rows = patches.shape[1]
    width = patches.shape[2]
    blk = lax.axis_index("blk")
    chip, core = blk // 2, blk % 2
    sources = lax.axis_size("seq")

    lane = core * (width - PAIR)
    shard = query_weight.shape[1]
    quarter = shard // 4
    pair = keyval_weight.shape[1]

    def half(weight, start, count):
        return lax.dynamic_slice(weight, (start, lane), (count, PAIR))

    depth, height = 8, sources // 8
    groups = [[y * depth + z for z in range(depth)] for y in range(height)]

    def copies(piece):
        return jnp.broadcast_to(piece[None], (depth,) + piece.shape)

    def along_z(spread):
        return lax.all_to_all(spread, "seq", 0, 0, axis_index_groups=groups, tiled=True)

    piece = jnp.concatenate(
        [
            half(query_weight.T, chip * quarter, quarter),
            half(output_weight, chip * quarter, quarter),
        ],
        axis=0,
    )
    piece, slab = copies(piece), copies(half(keyval_weight.T, 0, pair))
    piece, slab = after(piece, slab)
    spread, patches, recompute_rows = after(along_z(piece), patches, recompute_rows)
    keyval_own = along_z(slab).reshape(depth * pair, PAIR)
    cached = cached_keyval[0]
    cached_before, cached_after = neighbours(cached)
    slim = depth * quarter
    small = jnp.concatenate(
        [
            spread[:, :quarter].reshape(slim, PAIR),
            spread[:, quarter:].reshape(slim, PAIR),
        ],
        axis=0,
    )
    column = lax.axis_index("seq") // depth
    small = around(small, shift_y)
    query_own = jnp.concatenate([v[:slim] for v in small], axis=0)
    output_own = jnp.concatenate([v[slim:] for v in small], axis=0)
    query_own, output_own, keyval_own, cached_before, cached_after = after(
        query_own, output_own, keyval_own, cached_before, cached_after
    )
    keyval_parts = around(keyval_own, shift_y)
    query_part = around(query_own, shift)
    output_part = around(output_own, shift)
    query_other = [swap(w) for w in query_part]
    output_other = [swap(w) for w in output_part]
    column, query_own = after(column, query_own)
    m = lax.broadcasted_iota(jnp.int32, (width, width), 0)
    n = lax.broadcasted_iota(jnp.int32, (width, width), 1)

    def steps_of(place):
        return jnp.where(place == 2, 3, jnp.where(place == 3, 2, place))

    block = height * slim
    source_chip = (chip - steps_of(m // block) + 4) % 4
    source_column = (column - steps_of((m % block) // slim) + height) % height
    source = source_column * depth + (m % slim) // quarter
    natural = source * shard + source_chip * quarter + m % quarter
    reorder = (natural == n).astype(BF16)

    stream_in = patches[0].astype(F32)
    attention_in = layer_norm(stream_in).astype(BF16)
    picks = recompute_rows.shape[2]
    chosen = jnp.pad(recompute_rows[0, 0], (0, PICK - picks), constant_values=-1)
    row_of = lax.broadcasted_iota(jnp.int32, (PICK, rows), 1)
    chosen_rows = dot((chosen[:, None] == row_of).astype(BF16), attention_in).astype(BF16)
    segment_tag = jnp.repeat(group_segments[0], 4) + 1
    lines = rows // 128
    extra = jnp.concatenate(
        [
            jnp.pad(chosen[: PICK - lines, None].astype(BF16), ((0, 0), (0, 127))),
            segment_tag.astype(BF16).reshape(lines, 128),
        ],
        axis=0,
    )
    packet = jnp.concatenate([chosen_rows, extra], axis=1)
    packet_before, packet_after = neighbours(packet)

    def unpack(value):
        index = value[: PICK - lines, width].astype(jnp.int32)
        index = jnp.pad(index, (0, lines), constant_values=-1)
        return index, value[PICK - lines :, width:].reshape(rows).astype(jnp.int32)

    index_before, tag_before = unpack(packet_before)
    index_after, tag_after = unpack(packet_after)
    index = jnp.stack([index_before, chosen, index_after])
    key_tag = jnp.concatenate([tag_before, segment_tag, tag_after])


    keyval_full = jnp.zeros((sources * pair, PAIR), BF16)
    for steps, part in zip(ORDER, keyval_parts):
        place = ((column - steps + height) % height) * depth * pair
        keyval_full = lax.dynamic_update_slice(keyval_full, part, (place, 0))

    other_lane = (width - PAIR) - lane
    in_own = lax.dynamic_slice(attention_in, (0, lane), (rows, PAIR))
    in_other = lax.dynamic_slice(attention_in, (0, other_lane), (rows, PAIR))
    at = lax.broadcasted_iota(jnp.int32, in_other.shape, 1) + other_lane
    shared = (at >= width - PAIR) & (at < PAIR)
    in_other = jnp.where(shared, jnp.zeros_like(in_other), in_other)
    queries = jnp.concatenate(
        [dot_t(in_own, a) + dot_t(in_other, b) for a, b in zip(query_part, query_other)], axis=1
    ).astype(BF16)
    queries = dot(queries, reorder).astype(BF16)

    picked = jnp.concatenate([packet_before, packet, packet_after], axis=0)[:, :width]
    both = jnp.concatenate([picked, swap(picked)], axis=0)
    both = lax.dynamic_slice(both, (0, lane), (both.shape[0], PAIR))
    keep = (lax.broadcasted_iota(jnp.int32, both.shape, 1) >= core * (2 * PAIR - width)).astype(BF16)
    both, queries = after(both * keep, queries)
    partial = dot_t(both, keyval_full)
    renewed = (partial[: 3 * PICK] + swap(partial[3 * PICK :])).astype(BF16)

    context = attend(
        queries, cached_before, cached, cached_after, renewed, index, segment_tag[:, None], key_tag[None]
    )
    context = dot_t(context, reorder).astype(BF16)
    out_own = dot(context, jnp.concatenate(output_part, axis=0))
    out_other = dot(context, jnp.concatenate(output_other, axis=0))
    left = jnp.where(core == 0, out_own, out_other)
    right = jnp.where(core == 0, out_other, out_own)
    attended = jnp.concatenate([left, right[:, 2 * PAIR - width :]], axis=1)
    stream = (stream_in + attended).astype(BF16)

    normed = layer_norm(stream.astype(F32)).astype(BF16)
    behind, ahead = shift(normed, 1), shift(normed, 3)
    weights = (expand_weight, reduce_weight)

    def other_part(value):
        return swap(feed(value, *weights))

    def chip_part(value, from_other):
        return feed(value, *weights, from_other)

    top, bottom = shift(behind[: rows // 2], 1), shift(ahead[rows // 2 :], 3)
    other_1, other_2 = swap(behind), swap(ahead)
    from_1 = other_part(other_1)
    from_2 = other_part(other_2)
    top, bottom, from_1, from_2 = after(top, bottom, from_1, from_2)
    part_1 = chip_part(behind, from_1)
    back_1 = shift(part_1, 3)
    part_2 = chip_part(ahead, from_2)
    back_2 = shift(part_2, 1)
    other_3 = swap(jnp.concatenate([top, bottom], axis=0))
    opposite = jnp.concatenate([top, bottom], axis=0)
    normed, other_3, part_1, part_2 = after(normed, other_3, part_1, part_2)
    other_0 = swap(normed)
    from_3 = other_part(other_3)
    other_0, from_3 = after(other_0, from_3)
    from_0 = other_part(other_0)
    part_3 = chip_part(opposite, from_3)
    back_3 = shift(part_3, 2)
    from_0, part_3 = after(from_0, part_3)
    part_0 = chip_part(normed, from_0)
    total = part_0.astype(F32) + back_1.astype(F32) + back_2.astype(F32) + back_3.astype(F32)
    combined = stream.astype(F32) + total
    merged = layer_norm(combined).astype(BF16).reshape(rows // 4, 4 * width)

    destination = owners[0]
    count = destination.shape[0]
    capacity = 3 * count // sources
    same = destination[:, None] == destination[None, :]
    t = lax.broadcasted_iota(jnp.int32, (count, count), 0)
    u = lax.broadcasted_iota(jnp.int32, (count, count), 1)
    position = jnp.sum((same & (u < t)).astype(jnp.int32), axis=1)
    slot_index = (destination * capacity + position).reshape(8, count // 8)
    packs = jnp.stack(
        [2 * ((chip - j + 4) % 4) + c for j in ORDER for c in (core, 1 - core)]
    )
    slot_index = jnp.sum(
        jnp.where(packs[:, None, None] == jnp.arange(8)[None, :, None], slot_index[None], 0), axis=1
    ).reshape(count)
    dispatch = (
        slot_index[None, :] == lax.broadcasted_iota(jnp.int32, (sources * capacity, count), 0)
    ).astype(BF16)
    dispatch, merged = after(dispatch, merged)

    projected = []
    for value in around(merged, shift):
        pair = jnp.concatenate([value, swap(value)], axis=0)
        projected.append(dot(pair, merge_weight).astype(BF16))
    projected = jnp.concatenate(projected, axis=0)
    outgoing = dot(dispatch, projected).astype(BF16)
    outgoing = outgoing.reshape(sources, capacity, projected.shape[1])
    received = lax.all_to_all(outgoing, "seq", split_axis=0, concat_axis=0, tiled=True)
    return received[None]


def solution(mesh):
    return jax.shard_map(
        on_device,
        mesh=mesh,
        in_specs=(
            P("blk", "seq", None),
            P("blk", "seq"),
            P("blk", "seq", None),
            P("blk", "seq", None),
            P(None, "seq"),
            P(None, "seq"),
            P("seq", None),
            P(None, "blk"),
            P("blk", None),
            P(None, "blk"),
            P("seq", None),
        ),
        out_specs=P("seq", None, None, "blk"),
        check_vma=False,
    )
```

```python
import math

import jax
import jax.numpy as jnp
from jax import lax
from jax.experimental import pallas as pl
from jax.experimental.pallas import tpu as pltpu
from jax.sharding import PartitionSpec as P

HEADS = 16
HEAD = 88
PAIR = 768
PICK = 32
F32 = jnp.float32
BF16 = jnp.bfloat16
VM = pltpu.VMEM
ORDER = (0, 1, 3, 2)


def layer_norm(values):
    average = jnp.mean(values, axis=-1, keepdims=True)
    centered = values - average
    variance = jnp.mean(centered * centered, axis=-1, keepdims=True)
    return centered * lax.rsqrt(variance + 1e-06)


def swap(value):
    return lax.ppermute(value, "blk", [(b, b ^ 1) for b in range(8)])


def shift(value, steps):
    return lax.ppermute(value, "blk", [(b, (b + 2 * steps) % 8) for b in range(8)])


def neighbours(value):
    count = lax.axis_size("seq")
    up = [(i, i + 1) for i in range(count - 1)]
    before = lax.ppermute(value, "seq", up)
    after = lax.ppermute(value, "seq", [(j, i) for i, j in up])
    return before, after


def dot(a, b):
    return lax.dot_general(a, b, (((1,), (0,)), ((), ())), preferred_element_type=F32)


def dot_t(a, b):
    return lax.dot_general(a, b, (((1,), (1,)), ((), ())), preferred_element_type=F32)


def after(*values):
    return lax.optimization_barrier(values)


def shift_y(value, steps):
    count = lax.axis_size("seq")
    return lax.ppermute(value, "seq", [(s, (s + 8 * steps) % count) for s in range(count)])


def around(value, shift):
    behind, ahead = shift(value, 1), shift(value, 3)
    return [value, behind, ahead, across(behind, ahead, shift)]


def across(behind, ahead, shift):
    middle = behind.shape[0] // 2
    return jnp.concatenate([shift(behind[:middle], 1), shift(ahead[middle:], 3)], axis=0)


def feed_kernel(*refs):
    if len(refs) == 5:
        x_ref, e_ref, r_ref, add_ref, o_ref = refs
    else:
        x_ref, e_ref, r_ref, o_ref = refs
        add_ref = None
    units = e_ref.shape[1]
    x = x_ref[...]
    total = None
    for k in range(0, units, 256):
        inner = jnp.dot(x, e_ref[:, k:k+256], preferred_element_type=F32)
        hidden = (0.5 * inner * (1.0 + lax.erf(inner * math.sqrt(0.5)))).astype(BF16)
        part = jnp.dot(hidden, r_ref[k:k+256, :], preferred_element_type=F32)
        total = part if total is None else total + part
    if add_ref is not None:
        total = total + add_ref[...].astype(F32)
    o_ref[...] = total.astype(BF16)


def feed(x, e, r, add=None):
    args = (x, e, r) + (() if add is None else (add,))
    return pl.pallas_call(
        feed_kernel,
        out_shape=jax.ShapeDtypeStruct((x.shape[0], r.shape[1]), BF16),
        in_specs=[pl.BlockSpec(memory_space=VM)] * len(args),
        out_specs=pl.BlockSpec(memory_space=VM),
        compiler_params=pltpu.CompilerParams(vmem_limit_bytes=8 << 20),
        cost_estimate=pl.CostEstimate(
            flops=x.size,
            transcendentals=0,
            bytes_accessed=2 * (2 * x.size + e.size + r.size),
        ),
    )(*args)


def attend_kernel(q_ref, before_ref, own_ref, after_ref, fresh_ref, index_ref, qtag_ref, ktag_ref, o_ref, kv_ref, acc_ref):
    rows, width = q_ref.shape
    for b, old in enumerate((before_ref, own_ref, after_ref)):
        at = lax.broadcasted_iota(jnp.int32, (rows, PICK), 0)
        hit = (index_ref[b:b+1, :] == at).astype(F32)
        any_hit = jnp.max(hit, axis=1, keepdims=True) > 0.0
        hit = hit.astype(BF16)
        for k in range(0, 2*width, 256):
            new = jnp.dot(hit, fresh_ref[b*PICK:(b+1)*PICK, k:k+256], preferred_element_type=F32)
            kv_ref[b*rows:(b+1)*rows, k:k+256] = jnp.where(any_hit, new, old[:, k:k+256].astype(F32)).astype(BF16)
    allowed = qtag_ref[...] == ktag_ref[...]
    scale = 1.0 / math.sqrt(HEAD)
    for h in range(HEADS):
        lo = (HEAD*h)//128*128
        hi = -(-(HEAD*(h+1))//128)*128
        lane = lax.broadcasted_iota(jnp.int32, (rows, hi-lo), 1) + lo
        mine = (lane >= HEAD*h) & (lane < HEAD*(h+1))
        q = q_ref[:, lo:hi]
        q = jnp.where(mine, q.astype(F32), 0.0).astype(BF16)
        s = lax.dot_general(q, kv_ref[:, lo:hi], (((1,),(1,)),((),())), preferred_element_type=F32)
        s = jnp.where(allowed, s, -1e30)
        top = jnp.max(s, axis=1, keepdims=True)
        raised = jnp.exp((s - top) * scale)
        total = jnp.sum(raised, axis=1, keepdims=True)
        o = jnp.dot(raised.astype(BF16), kv_ref[:, width+lo:width+hi], preferred_element_type=F32)
        o = o / total
        acc_ref[:, lo:hi] = jnp.where(mine, o, acc_ref[:, lo:hi])
    o_ref[...] = acc_ref[...].astype(BF16)


def attend(q, before, own, after, fresh, index, qtag, ktag):
    rows, width = q.shape
    return pl.pallas_call(
        attend_kernel,
        out_shape=jax.ShapeDtypeStruct((rows, width), BF16),
        in_specs=[pl.BlockSpec(memory_space=VM)] * 8,
        out_specs=pl.BlockSpec(memory_space=VM),
        scratch_shapes=[VM((3*rows, 2*width), BF16), VM((rows, width), F32)],
        compiler_params=pltpu.CompilerParams(vmem_limit_bytes=24 << 20),
        cost_estimate=pl.CostEstimate(
            flops=12 * rows * rows * width,
            transcendentals=3 * HEADS * rows * rows,
            bytes_accessed=2 * (2 * q.size + 3 * own.size),
        ),
    )(q, before, own, after, fresh, index, qtag, ktag)


def on_device(
    patches,
    group_segments,
    cached_keyval,
    recompute_rows,
    query_weight,
    keyval_weight,
    output_weight,
    expand_weight,
    reduce_weight,
    merge_weight,
    owners,
):
    rows = patches.shape[1]
    width = patches.shape[2]
    blk = lax.axis_index("blk")
    chip, core = blk // 2, blk % 2
    sources = lax.axis_size("seq")

    lane = core * (width - PAIR)
    shard = query_weight.shape[1]
    quarter = shard // 4
    pair = keyval_weight.shape[1]

    def half(weight, start, count):
        return lax.dynamic_slice(weight, (start, lane), (count, PAIR))

    depth, height = 8, sources // 8
    groups = [[y * depth + z for z in range(depth)] for y in range(height)]

    def copies(piece):
        return jnp.broadcast_to(piece[None], (depth,) + piece.shape)

    def along_z(spread):
        return lax.all_to_all(spread, "seq", 0, 0, axis_index_groups=groups, tiled=True)

    piece = jnp.concatenate(
        [
            half(query_weight.T, chip * quarter, quarter),
            half(output_weight, chip * quarter, quarter),
        ],
        axis=0,
    )
    piece, slab = copies(piece), copies(half(keyval_weight.T, 0, pair))
    piece, slab, patches, recompute_rows = after(piece, slab, patches, recompute_rows)
    spread = along_z(piece)
    keyval_own = along_z(slab).reshape(depth * pair, PAIR)
    cached = cached_keyval[0]
    cached_before, cached_after = neighbours(cached)
    slim = depth * quarter
    small = jnp.concatenate(
        [
            spread[:, :quarter].reshape(slim, PAIR),
            spread[:, quarter:].reshape(slim, PAIR),
        ],
        axis=0,
    )
    column = lax.axis_index("seq") // depth
    small = around(small, shift_y)
    query_own = jnp.concatenate([v[:slim] for v in small], axis=0)
    output_own = jnp.concatenate([v[slim:] for v in small], axis=0)
    query_own, output_own, keyval_own, cached_before, cached_after = after(
        query_own, output_own, keyval_own, cached_before, cached_after
    )
    near = [shift(v, steps) for v in (query_own, output_own) for steps in (1, 3)]
    near = after(*near, shift_y(keyval_own, 1), shift_y(keyval_own, 3))
    keyval_parts = [keyval_own, *near[4:], across(*near[4:], shift_y)]
    query_part = [query_own, *near[:2], across(*near[:2], shift)]
    output_part = [output_own, *near[2:4], across(*near[2:4], shift)]
    query_other = [swap(w) for w in query_part]
    output_other = [swap(w) for w in output_part]
    column, query_own = after(column, query_own)
    m = lax.broadcasted_iota(jnp.int32, (width, width), 0)
    n = lax.broadcasted_iota(jnp.int32, (width, width), 1)

    def steps_of(place):
        return jnp.where(place == 2, 3, jnp.where(place == 3, 2, place))

    block = height * slim
    source_chip = (chip - steps_of(m // block) + 4) % 4
    source_column = (column - steps_of((m % block) // slim) + height) % height
    source = source_column * depth + (m % slim) // quarter
    natural = source * shard + source_chip * quarter + m % quarter
    reorder = (natural == n).astype(BF16)

    stream_in = patches[0].astype(F32)
    attention_in = layer_norm(stream_in).astype(BF16)
    picks = recompute_rows.shape[2]
    chosen = jnp.pad(recompute_rows[0, 0], (0, PICK - picks), constant_values=-1)
    row_of = lax.broadcasted_iota(jnp.int32, (PICK, rows), 1)
    chosen_rows = dot((chosen[:, None] == row_of).astype(BF16), attention_in).astype(BF16)
    segment_tag = jnp.repeat(group_segments[0], 4) + 1
    lines = rows // 128
    extra = jnp.concatenate(
        [
            jnp.pad(chosen[: PICK - lines, None].astype(BF16), ((0, 0), (0, 127))),
            segment_tag.astype(BF16).reshape(lines, 128),
        ],
        axis=0,
    )
    packet = jnp.concatenate([chosen_rows, extra], axis=1)
    packet_before, packet_after = neighbours(packet)

    def unpack(value):
        index = value[: PICK - lines, width].astype(jnp.int32)
        index = jnp.pad(index, (0, lines), constant_values=-1)
        return index, value[PICK - lines :, width:].reshape(rows).astype(jnp.int32)

    index_before, tag_before = unpack(packet_before)
    index_after, tag_after = unpack(packet_after)
    index = jnp.stack([index_before, chosen, index_after])
    key_tag = jnp.concatenate([tag_before, segment_tag, tag_after])


    keyval_full = jnp.zeros((sources * pair, PAIR), BF16)
    for steps, part in zip(ORDER, keyval_parts):
        place = ((column - steps + height) % height) * depth * pair
        keyval_full = lax.dynamic_update_slice(keyval_full, part, (place, 0))

    other_lane = (width - PAIR) - lane
    in_own = lax.dynamic_slice(attention_in, (0, lane), (rows, PAIR))
    in_other = lax.dynamic_slice(attention_in, (0, other_lane), (rows, PAIR))
    at = lax.broadcasted_iota(jnp.int32, in_other.shape, 1) + other_lane
    shared = (at >= width - PAIR) & (at < PAIR)
    in_other = jnp.where(shared, jnp.zeros_like(in_other), in_other)
    queries = jnp.concatenate(
        [dot_t(in_own, a) + dot_t(in_other, b) for a, b in zip(query_part, query_other)], axis=1
    ).astype(BF16)
    queries = dot(queries, reorder).astype(BF16)

    picked = jnp.concatenate([packet_before, packet, packet_after], axis=0)[:, :width]
    both = jnp.concatenate([picked, swap(picked)], axis=0)
    both = lax.dynamic_slice(both, (0, lane), (both.shape[0], PAIR))
    keep = (lax.broadcasted_iota(jnp.int32, both.shape, 1) >= core * (2 * PAIR - width)).astype(BF16)
    both, queries, output_part[3] = after(both * keep, queries, output_part[3])
    partial = dot_t(both, keyval_full)
    renewed = (partial[: 3 * PICK] + swap(partial[3 * PICK :])).astype(BF16)

    context = attend(
        queries, cached_before, cached, cached_after, renewed, index, segment_tag[:, None], key_tag[None]
    )
    context = dot_t(context, reorder).astype(BF16)
    out_own = dot(context, jnp.concatenate(output_part, axis=0))
    out_other = dot(context, jnp.concatenate(output_other, axis=0))
    left = jnp.where(core == 0, out_own, out_other)
    right = jnp.where(core == 0, out_other, out_own)
    attended = jnp.concatenate([left, right[:, 2 * PAIR - width :]], axis=1)
    stream = (stream_in + attended).astype(BF16)

    normed = layer_norm(stream.astype(F32)).astype(BF16)
    behind, ahead = shift(normed, 1), shift(normed, 3)
    weights = (expand_weight, reduce_weight)

    def other_part(value):
        return swap(feed(value, *weights))

    def chip_part(value, from_other):
        return feed(value, *weights, from_other)

    top, bottom = shift(behind[: rows // 2], 1), shift(ahead[rows // 2 :], 3)
    other_1, other_2 = swap(behind), swap(ahead)
    from_1 = other_part(other_1)
    from_2 = other_part(other_2)
    part_1 = chip_part(behind, from_1)
    back_1 = shift(part_1, 3)
    part_2 = chip_part(ahead, from_2)
    back_2 = shift(part_2, 1)
    top, bottom, normed, part_1, part_2 = after(top, bottom, normed, part_1, part_2)
    opposite = jnp.concatenate([top, bottom], axis=0)
    other_3 = swap(opposite)
    other_0 = swap(normed)
    from_3 = other_part(other_3)
    other_0, from_3 = after(other_0, from_3)
    from_0 = other_part(other_0)
    part_3 = chip_part(opposite, from_3)
    back_3 = shift(part_3, 2)
    from_0, part_3 = after(from_0, part_3)
    part_0 = chip_part(normed, from_0)
    total = part_0.astype(F32) + back_1.astype(F32) + back_2.astype(F32) + back_3.astype(F32)
    combined = stream.astype(F32) + total
    merged = layer_norm(combined).astype(BF16).reshape(rows // 4, 4 * width)

    destination = owners[0]
    count = destination.shape[0]
    capacity = 3 * count // sources
    same = destination[:, None] == destination[None, :]
    t = lax.broadcasted_iota(jnp.int32, (count, count), 0)
    u = lax.broadcasted_iota(jnp.int32, (count, count), 1)
    position = jnp.sum((same & (u < t)).astype(jnp.int32), axis=1)
    slot_index = (destination * capacity + position).reshape(8, count // 8)
    packs = jnp.stack(
        [2 * ((chip - j + 4) % 4) + c for j in ORDER for c in (core, 1 - core)]
    )
    slot_index = jnp.sum(
        jnp.where(packs[:, None, None] == jnp.arange(8)[None, :, None], slot_index[None], 0), axis=1
    ).reshape(count)
    dispatch = (
        slot_index[None, :] == lax.broadcasted_iota(jnp.int32, (sources * capacity, count), 0)
    ).astype(BF16)
    dispatch, merged = after(dispatch, merged)

    projected = []
    for value in around(merged, shift):
        pair = jnp.concatenate([value, swap(value)], axis=0)
        projected.append(dot(pair, merge_weight).astype(BF16))
    projected = jnp.concatenate(projected, axis=0)
    outgoing = dot(dispatch, projected).astype(BF16)
    outgoing = outgoing.reshape(sources, capacity, projected.shape[1])
    received = lax.all_to_all(outgoing, "seq", split_axis=0, concat_axis=0, tiled=True)
    return received[None]


def solution(mesh):
    return jax.shard_map(
        on_device,
        mesh=mesh,
        in_specs=(
            P("blk", "seq", None),
            P("blk", "seq"),
            P("blk", "seq", None),
            P("blk", "seq", None),
            P(None, "seq"),
            P(None, "seq"),
            P("seq", None),
            P(None, "blk"),
            P("blk", None),
            P(None, "blk"),
            P("seq", None),
        ),
        out_specs=P("seq", None, None, "blk"),
        check_vma=False,
    )
```
